128 devices in a mesh: thinker: 4 (over z), seq: 32 (over y, x, core).
Axes of the slice: x: 4, y: 4, z: 4, core: 2. Of those that a mesh axis runs over, the one named last changes fastest.
Arguments:
- queries: bfloat16 [4, 4096, 2048], P('thinker', 'seq'), may hold values from -6 to 6
- keys: bfloat16 [4, 4096, 512], P('thinker', 'seq'), may hold values from -6 to 6
- values: bfloat16 [4, 4096, 512], P('thinker', 'seq'), may hold values from -6 to 6
- forward_out: bfloat16 [4, 4096, 2048], P('thinker', 'seq'), may hold values from -2 to 2
- logsumexp: float32 [4, 16, 4096], P('thinker', None, 'seq'), may hold values from -1 to 16, as said below
- upstream: bfloat16 [128, 128, 2048], P(None, ('thinker', 'seq')), may hold values from -6 to 6
- lengths: int32 [4], replicated, may hold values from 512 to 4096, as said below
- sibling_mask: int32 [4, 3, 32], P('thinker', None, 'seq'), may hold values from 0 to 1, as said below
Outputs:
- query_grad: bfloat16 [4, 4096, 2048], P('thinker', 'seq')
- key_grad: bfloat16 [4, 4096, 512], P('thinker', 'seq')
- value_grad: bfloat16 [4, 4096, 512], P('thinker', 'seq')
The draws below stay inside these ranges and needn't reach their ends.
Inputs may be any that keep to these rules, and one draw needn't show every extreme that they name: lengths[t] valid positions stand at the start of thinker t's trace; two thinkers have exactly 4096, one exactly 512. sibling_mask[t, r, b] = 1 where query block b of thinker t reads the recent tokens of thinker (t + r + 1) % 4; the two thinkers of length 4096 read each other in the blocks of the last 128 positions. `logsumexp`: rows of positions past a trace's length carry arbitrary values.
All inputs are finite; a program needn't handle non-finite values.
Results may differ from the reference program's by a relative error of at most 0.014.
Values may be sent and summed in bfloat16 or wider, within the bound.
No kernel may reach another device: no remote copies, remote signals or barrier semaphores. Data moves between devices by JAX's collectives and lax.ppermute only.
A program may use at most 128 MiB of HBM per device.

```python
import jax
import jax.numpy as jnp
from jax import lax

TOK_DEV = 128
HEADS = 16
KV_HEADS = 4
HD = 128
BLOCK = 128
THINKERS = 4
SHARDS = 32
LENGTH = 4096
GROUP = 4
QW = 2048
KW = 512
N_SEQ = 32


def shared_draw(key):
    length = TOK_DEV * N_SEQ
    blocks = length // BLOCK
    order = jax.random.permutation(jax.random.fold_in(key, 101), THINKERS)
    spans = jax.random.randint(jax.random.fold_in(key, 102), (THINKERS,), length // 8, length + 1)
    spans = spans.at[order[0]].set(length)
    spans = spans.at[order[1]].set(length)
    spans = spans.at[order[2]].set(length // 8)
    visible = jax.random.randint(jax.random.fold_in(key, 103), (THINKERS, THINKERS - 1, blocks), 0, 2)
    block_ids = jnp.arange(blocks, dtype=jnp.int32)
    last_blocks = block_ids >= blocks - TOK_DEV // BLOCK
    first_reads = (order[1] - order[0] - 1) % THINKERS
    second_reads = (order[0] - order[1] - 1) % THINKERS
    thinker_ids = jnp.arange(THINKERS, dtype=jnp.int32)[:, None, None]
    offset_ids = jnp.arange(THINKERS - 1, dtype=jnp.int32)[None, :, None]
    forced = (thinker_ids == order[0]) & (offset_ids == first_reads) | (thinker_ids == order[1]) & (offset_ids == second_reads)
    forced = forced & last_blocks[None, None, :]
    visible = jnp.where(forced, 1, visible)
    return (spans.astype(jnp.int32), visible.astype(jnp.int32))


def draw_lengths(key, part):
    return shared_draw(key)[0]


def draw_sibling_mask(key, part):
    return shared_draw(key)[1]


def draw_logsumexp(key, part):
    length = TOK_DEV * N_SEQ
    spans, visible = shared_draw(key)
    positions = jnp.arange(length, dtype=jnp.int32)
    counts = jnp.where(positions[None, :] < spans[:, None], positions[None, :] + 1, 0)
    block_ids = positions // BLOCK
    lowest = jnp.maximum(positions - TOK_DEV + 1, 0)
    thinker_ids = jnp.arange(THINKERS, dtype=jnp.int32)
    for offset in range(1, THINKERS):
        sibling_len = spans[(thinker_ids + offset) % THINKERS]
        highest = jnp.minimum(positions[None, :], sibling_len[:, None] - 1)
        reach = jnp.maximum(highest - lowest[None, :] + 1, 0)
        counts = counts + visible[:, offset - 1][:, block_ids] * reach
    base = 0.5 * jnp.log(jnp.maximum(counts, 1).astype(jnp.float32)) + 0.5
    noise = jax.random.uniform(jax.random.fold_in(key, 104), (THINKERS, HEADS, length), jnp.float32, -0.5, 0.5)
    return base[:, None, :] + noise


def block_levels(rng, shape, cuts, smallest, top_value):
    def one(axis_at, blocks):
        draws = jax.random.uniform(jax.random.fold_in(jax.random.fold_in(rng, 6), axis_at), (blocks,), jnp.float32, smallest / len(cuts), top_value / len(cuts))
        return jnp.repeat(jnp.exp(draws), shape[axis_at] // blocks).reshape((-1,) + (1,) * (len(shape) - axis_at - 1))

    level = one(*cuts[0])
    for cut in cuts[1:]:
        level = level * one(*cut)
    return level


def scatter_about(stream_key, extent, width, most, pieces=(), kind=jnp.bfloat16):
    array = jax.random.normal(stream_key, extent, jnp.float32) * width
    if len(pieces) > 0:
        array = block_levels(stream_key, extent, pieces, -0.22, 0.18) * array
    return jnp.clip(array, min=-most, max=most).astype(kind)


def setup_inputs(seed: int = 0) -> dict:
    streams_of = jax.random.split(jax.random.key(seed), 9)
    return {
        "queries": scatter_about(streams_of[0], (THINKERS, LENGTH, QW), 1.0, 6.0, ((0, 4), (1, 32))),
        "keys": scatter_about(streams_of[1], (THINKERS, LENGTH, KW), 1.0, 6.0, ((0, 4), (1, 32))),
        "values": scatter_about(streams_of[2], (THINKERS, LENGTH, KW), 1.0, 6.0, ((0, 4), (1, 32))),
        "forward_out": scatter_about(streams_of[3], (THINKERS, LENGTH, QW), 0.3, 2.0, ((0, 4), (1, 32))),
        "logsumexp": draw_logsumexp(jax.random.fold_in(streams_of[8], 71), 0),
        "upstream": scatter_about(streams_of[5], (TOK_DEV, THINKERS * SHARDS, QW), 1.0, 6.0, ((1, 128),)),
        "lengths": draw_lengths(jax.random.fold_in(streams_of[8], 71), 0),
        "sibling_mask": draw_sibling_mask(jax.random.fold_in(streams_of[8], 71), 0),
    }


def pair_grads(query_heads, upstream_heads, lse_heads, delta_heads, key_rows, value_rows, allowed, factor):
    count = key_rows.shape[0]
    kv_heads = query_heads.shape[1]
    head_dim = query_heads.shape[3]
    query_wide = query_heads.astype(jnp.float32)
    upstream_wide = upstream_heads.astype(jnp.float32)
    key_heads = key_rows.reshape(count, kv_heads, head_dim).astype(jnp.float32)
    value_heads = value_rows.reshape(count, kv_heads, head_dim).astype(jnp.float32)
    scores = jnp.einsum("ikgd,jkd->kgij", query_wide, key_heads) * factor
    probs = jnp.where(allowed, jnp.exp(scores - lse_heads[..., None]), 0.0)
    dprobs = jnp.einsum("ikgd,jkd->kgij", upstream_wide, value_heads)
    dscores = probs * (dprobs - delta_heads[..., None])
    probs_low = lax.optimization_barrier(probs.astype(jnp.bfloat16)).astype(jnp.float32)
    dscores_low = lax.optimization_barrier(dscores.astype(jnp.bfloat16)).astype(jnp.float32)
    value_part = jnp.einsum("kgij,ikgd->jkd", probs_low, upstream_wide)
    key_part = jnp.einsum("kgij,ikgd->jkd", dscores_low, query_wide) * factor
    query_part = jnp.einsum("kgij,jkd->ikgd", dscores_low, key_heads) * factor
    rows = query_heads.shape[0]
    return query_part.reshape(rows, -1), key_part.reshape(count, -1), value_part.reshape(count, -1)


def round_low(term):
    return lax.optimization_barrier(term.astype(jnp.bfloat16)).astype(jnp.float32)


def reference(queries, keys, values, forward_out, logsumexp, upstream, lengths, sibling_mask):
    length = TOK_DEV * N_SEQ
    factor = HD ** -0.5
    kwidth = KV_HEADS * HD
    grad_out = upstream.reshape(THINKERS, length, HEADS * HD)
    delta = jnp.sum((grad_out.astype(jnp.float32) * forward_out.astype(jnp.float32)).reshape(THINKERS, length, KV_HEADS, GROUP, HD), axis=-1)
    positions = jnp.arange(length, dtype=jnp.int32)
    local = jnp.arange(TOK_DEV, dtype=jnp.int32)
    window = jnp.arange(2 * TOK_DEV, dtype=jnp.int32)
    key_grad = jnp.zeros((THINKERS, length, kwidth), jnp.float32)
    value_grad = jnp.zeros((THINKERS, length, kwidth), jnp.float32)
    padded_keys = [jnp.concatenate([jnp.zeros((TOK_DEV, kwidth), keys.dtype), keys[u]], axis=0) for u in range(THINKERS)]
    padded_values = [jnp.concatenate([jnp.zeros((TOK_DEV, kwidth), values.dtype), values[u]], axis=0) for u in range(THINKERS)]
    query_list = []
    for thinker in range(THINKERS):
        own_length = lengths[thinker]

        def shard_step(carry, shard):
            key_acc, value_acc = carry
            start = (shard * TOK_DEV).astype(jnp.int32)
            query_pos = start + local
            live = query_pos < own_length
            query_heads = lax.dynamic_slice_in_dim(queries[thinker], start, TOK_DEV, 0).reshape(TOK_DEV, KV_HEADS, GROUP, HD)
            upstream_heads = lax.dynamic_slice_in_dim(grad_out[thinker], start, TOK_DEV, 0).reshape(TOK_DEV, KV_HEADS, GROUP, HD)
            lse_heads = lax.dynamic_slice_in_dim(logsumexp[thinker], start, TOK_DEV, 1).reshape(KV_HEADS, GROUP, TOK_DEV)
            delta_heads = jnp.transpose(lax.dynamic_slice_in_dim(delta[thinker], start, TOK_DEV, 0), (1, 2, 0))
            allowed = (positions[None, :] <= query_pos[:, None]) & live[:, None] & (positions[None, :] < own_length)
            query_part, key_part, value_part = pair_grads(query_heads, upstream_heads, lse_heads, delta_heads, keys[thinker], values[thinker], allowed, factor)
            block_ids = query_pos // BLOCK
            key_pos = start - TOK_DEV + window
            near = (key_pos[None, :] <= query_pos[:, None]) & (key_pos[None, :] > query_pos[:, None] - TOK_DEV) & (key_pos[None, :] >= 0) & live[:, None]
            sibling_keys = []
            sibling_values = []
            for offset in range(1, THINKERS):
                sibling = (thinker + offset) % THINKERS
                visible = sibling_mask[thinker, offset - 1][block_ids] == 1
                allowed_sibling = near & visible[:, None] & (key_pos[None, :] < lengths[sibling])
                key_rows = lax.dynamic_slice_in_dim(padded_keys[sibling], start, 2 * TOK_DEV, 0)
                value_rows = lax.dynamic_slice_in_dim(padded_values[sibling], start, 2 * TOK_DEV, 0)
                extra_query, extra_key, extra_value = pair_grads(query_heads, upstream_heads, lse_heads, delta_heads, key_rows, value_rows, allowed_sibling, factor)
                query_part = query_part + extra_query
                sibling_keys.append(extra_key)
                sibling_values.append(extra_value)
            new_carry = (key_acc + round_low(key_part), value_acc + round_low(value_part))
            return new_carry, (query_part, jnp.stack(sibling_keys), jnp.stack(sibling_values))

        empty = jnp.zeros((length, kwidth), jnp.float32)
        (own_key, own_value), (query_parts, sib_key, sib_value) = lax.scan(shard_step, (empty, empty), jnp.arange(N_SEQ, dtype=jnp.int32))
        query_list.append(query_parts.reshape(length, HEADS * HD))
        key_grad = key_grad.at[thinker].add(own_key)
        value_grad = value_grad.at[thinker].add(own_value)
        tail = jnp.zeros((TOK_DEV, kwidth), jnp.float32)
        for offset in range(1, THINKERS):
            sibling = (thinker + offset) % THINKERS
            part_key = sib_key[:, offset - 1]
            part_value = sib_value[:, offset - 1]
            upper_key = part_key[:, TOK_DEV:].reshape(length, kwidth)
            lower_key = part_key[:, :TOK_DEV].reshape(length, kwidth)
            upper_value = part_value[:, TOK_DEV:].reshape(length, kwidth)
            lower_value = part_value[:, :TOK_DEV].reshape(length, kwidth)
            key_grad = key_grad.at[sibling].add(upper_key + jnp.concatenate([lower_key[TOK_DEV:], tail], axis=0))
            value_grad = value_grad.at[sibling].add(upper_value + jnp.concatenate([lower_value[TOK_DEV:], tail], axis=0))
    query_grad = jnp.stack(query_list).astype(jnp.bfloat16)
    return query_grad, key_grad.astype(jnp.bfloat16), value_grad.astype(jnp.bfloat16)
```

```python
import jax
import jax.numpy as jnp
from jax import lax
from jax.experimental import pallas as pl
from jax.experimental.pallas import tpu as pltpu
from jax.sharding import Mesh, PartitionSpec as P

B = 128
HD = 128
GROUP = 4
HEADS = 4
ROWS = GROUP * B
STAT = 2 * ROWS
PAY = STAT + 32
FACTOR = HD**-0.5
LOG2E = 1.4426950408889634
SCALE = FACTOR * LOG2E
DEAD = 1e30
F32 = jnp.float32
BF16 = jnp.bfloat16
SEQ = ("y", "x", "c")
VMEM = pl.BlockSpec(memory_space=pltpu.VMEM)
SMEM = pl.BlockSpec(memory_space=pltpu.SMEM)


def nt(a, b):
    return lax.dot_general(a, b, (((1,), (1,)), ((), ())), preferred_element_type=F32)


def nn(a, b):
    return jnp.dot(a, b, preferred_element_type=F32)


def call(kernel, name, outs, n_smem, n_vmem, scratch=(), aliases=None):
    return pl.pallas_call(
        kernel,
        out_shape=outs,
        in_specs=[SMEM] * n_smem + [VMEM] * n_vmem,
        out_specs=jax.tree.map(lambda _: VMEM, outs),
        scratch_shapes=list(scratch),
        input_output_aliases=aliases or {},
        compiler_params=pltpu.CompilerParams(vmem_limit_bytes=48 << 20),
        name=name,
    )


def shape(dims, dtype):
    return jax.ShapeDtypeStruct(dims, dtype)


def split_kv(k_ref, v_ref, out_ref):
    for h in range(HEADS):
        out_ref[h, 0] = k_ref[:, h * HD : (h + 1) * HD]
        out_ref[h, 1] = v_ref[:, h * HD : (h + 1) * HD]


def three(x):
    high = x.astype(BF16)
    rest = x - high.astype(F32)
    mid = rest.astype(BF16)
    low = (rest - mid.astype(F32)).astype(BF16)
    return [high.astype(F32), mid.astype(F32), low.astype(F32)]


def payload(g_ref, o_ref, q_ref, lse_ref, out_ref):
    for c in range(HEADS):
        deltas = []
        for g in range(GROUP):
            cols = slice((c * GROUP + g) * HD, (c * GROUP + g + 1) * HD)
            grad = g_ref[:, cols]
            out_ref[c, g * B : (g + 1) * B, :] = q_ref[:, cols]
            out_ref[c, ROWS + g * B : ROWS + (g + 1) * B, :] = grad
            prod = grad.astype(F32) * o_ref[:, cols].astype(F32)
            deltas.append(jnp.sum(prod.T, axis=0, keepdims=True))
        delta = jnp.concatenate(deltas, axis=0)
        lse = lse_ref[c * GROUP : (c + 1) * GROUP, :]
        rows = three(delta) + three(lse) + [jnp.zeros((8, B), F32)]
        out_ref[c, STAT:PAY, :] = jnp.concatenate(rows, axis=0).astype(BF16)


def load_stats(p_ref, stat_ref, i, start, length):
    raw = p_ref[i, STAT:PAY, :].astype(F32)
    delta = raw[0:4] + raw[4:8] + raw[8:12]
    lse = raw[12:16] + raw[16:20] + raw[20:24]
    pos = start + lax.broadcasted_iota(jnp.int32, (GROUP, B), 1)
    lse = jnp.where(pos < length, lse * LOG2E, DEAD)
    for g in range(GROUP):
        stat_ref[i, 0:1, g * B : (g + 1) * B] = delta[g : g + 1]
        stat_ref[i, 1:2, g * B : (g + 1) * B] = lse[g : g + 1]


def make_own(dist, first, last):
    def kernel(*refs):
        len_ref, p_ref, km_ref, ko_ref = refs[:4]
        refs = refs[4:]
        if not first:
            dq_in = refs[0]
            refs = refs[1:]
        dm_ref, do_ref, dq_out, stat_ref, kt_ref, dk_ref, dv_ref = refs[:7]
        acc_ref = refs[7] if last else dq_out
        thinker = lax.axis_index("z")
        chip = lax.axis_index("x")
        core = lax.axis_index("c")
        length = len_ref[thinker]
        for i in range(4):
            load_stats(p_ref, stat_ref, i, (8 * i + 2 * chip + core) * B, length)
        if first:
            acc_ref[...] = jnp.zeros_like(acc_ref)
        else:
            acc_ref[...] = dq_in[...]
        source = lax.rem(chip + 4 - dist, 4)
        below = (source < chip).astype(jnp.int32)

        def key_tile(m, carry):
            keys = jnp.concatenate([km_ref[m, 0], ko_ref[m, 0]], axis=0)
            vals = jnp.concatenate([km_ref[m, 1], ko_ref[m, 1]], axis=0)
            kt_ref[...] = keys.T
            dk_ref[...] = jnp.zeros_like(dk_ref)
            dv_ref[...] = jnp.zeros_like(dv_ref)

            def query_block(i, inner):
                q = p_ref[i, 0:ROWS, :]
                grad = p_ref[i, ROWS:STAT, :]
                prob = jnp.exp2(nt(keys, q) * SCALE - stat_ref[i, 1:2, :])
                if dist == 0:
                    row = lax.broadcasted_iota(jnp.int32, (2 * B, ROWS), 0)
                    col = lax.broadcasted_iota(jnp.int32, (2 * B, ROWS), 1)
                    half = row // B
                    where_key = jnp.where(core == 0, half, 1 - half) * B + row % B
                    limit = core * B + col % B + jnp.where(i > m, 4 * B, 0)
                    prob = jnp.where(where_key <= limit, prob, 0.0)
                diff = nt(vals, grad) - stat_ref[i, 0:1, :]
                ds = (prob * diff).astype(BF16)
                dv_ref[...] += nn(prob.astype(BF16), grad)
                dk_ref[...] += nn(ds, q)
                acc_ref[i] += nn(kt_ref[...], ds)
                return inner

            lo = m if dist == 0 else m + 1 - below
            lax.fori_loop(lo, 4, query_block, 0)
            dk = (dk_ref[...] * FACTOR).astype(BF16)
            dv = dv_ref[...].astype(BF16)
            dm_ref[m, 0] = dk[:B]
            dm_ref[m, 1] = dv[:B]
            do_ref[m, 0] = dk[B:]
            do_ref[m, 1] = dv[B:]
            return carry

        lax.fori_loop(0, 4, key_tile, 0)
        if last:
            for i in range(4):
                dq_out[i] = (acc_ref[i].T * FACTOR).astype(BF16)

    kv = shape((4, 2, B, HD), BF16)
    dq = shape((4, ROWS, HD), BF16) if last else shape((4, HD, ROWS), F32)
    scratch = [
        pltpu.VMEM((4, 2, ROWS), F32),
        pltpu.VMEM((HD, 2 * B), BF16),
        pltpu.VMEM((2 * B, HD), F32),
        pltpu.VMEM((2 * B, HD), F32),
    ]
    if last:
        scratch.append(pltpu.VMEM((4, HD, ROWS), F32))
    return call(kernel, f"own{dist}", (kv, kv, dq), 1, 3 if first else 4, scratch)


def sibling_kernel(len_ref, mask_ref, p_ref, *refs):
    cur, prev, dcur, dprev = refs[0:3], refs[3:6], refs[6:9], refs[9:12]
    dq_out, stat_ref, acc_ref = refs[12:15]
    thinker = lax.axis_index("z")
    block = lax.axis_index("y") * 8 + lax.axis_index("x") * 2 + lax.axis_index("c")
    length = len_ref[thinker]
    for h in range(HEADS):
        load_stats(p_ref, stat_ref, h, block * B, length)

    def head(h, carry):
        acc_ref[...] = jnp.zeros_like(acc_ref)
        for d in (1, 2, 3):
            other = lax.rem(thinker + 4 - d, 4)
            top = len_ref[other] - (block - 1) * B
            low = jnp.where(block == 0, B, 0)
            live = (mask_ref[3 - d] == 1) & (block * B < length) & (top > 0)
            n = d - 1

            @pl.when(live)
            def _():
                keys = jnp.concatenate([prev[n][h, 0], cur[n][h, 0]], axis=0)
                vals = jnp.concatenate([prev[n][h, 1], cur[n][h, 1]], axis=0)
                q = p_ref[h, 0:ROWS, :]
                grad = p_ref[h, ROWS:STAT, :]
                row = lax.broadcasted_iota(jnp.int32, (2 * B, ROWS), 0)
                col = lax.broadcasted_iota(jnp.int32, (1, ROWS), 1) % B
                lower = jnp.maximum(col, low - 1)
                upper = jnp.minimum(col + B, top - 1)
                prob = jnp.exp2(nt(keys, q) * SCALE - stat_ref[h, 1:2, :])
                prob = jnp.where((row > lower) & (row <= upper), prob, 0.0)
                diff = nt(vals, grad) - stat_ref[h, 0:1, :]
                ds = (prob * diff).astype(BF16)
                dv = nn(prob.astype(BF16), grad).astype(BF16)
                dk = (nn(ds, q) * FACTOR).astype(BF16)
                acc_ref[...] += nn(keys.T, ds)
                dprev[n][h, 0] = dk[:B]
                dprev[n][h, 1] = dv[:B]
                dcur[n][h, 0] = dk[B:]
                dcur[n][h, 1] = dv[B:]

            @pl.when(jnp.logical_not(live))
            def _():
                dprev[n][h] = jnp.zeros((2, B, HD), BF16)
                dcur[n][h] = jnp.zeros((2, B, HD), BF16)

        dq_out[h] = acc_ref[...].T * FACTOR
        return carry

    lax.fori_loop(0, HEADS, head, 0)


def finish(dq_ref, sq_ref, kv_ref, s1_ref, s2_ref, s3_ref, q_out, k_out, v_out):
    for c in range(HEADS):
        for g in range(GROUP):
            rows = slice(g * B, (g + 1) * B)
            cols = slice((c * GROUP + g) * HD, (c * GROUP + g + 1) * HD)
            q_out[:, cols] = (dq_ref[c, rows, :].astype(F32) + sq_ref[c, rows, :]).astype(BF16)
        cols = slice(c * HD, (c + 1) * HD)
        for n, out in ((0, k_out), (1, v_out)):
            total = kv_ref[c, n].astype(F32) + s1_ref[c, n].astype(F32)
            total = total + s2_ref[c, n].astype(F32) + s3_ref[c, n].astype(F32)
            out[:, cols] = total.astype(BF16)


def ring(x, axis, step, count):
    return lax.ppermute(x, axis, [(j, (j + step) % count) for j in range(count)])


def shards(queries, keys, values, forward_out, logsumexp, upstream, lengths, sibling_mask):
    kv = shape((4, 2, B, HD), BF16)
    kv_pos = call(split_kv, "split_kv", kv, 0, 2)(keys[0], values[0])
    cur = [ring(kv_pos, "z", d, 4) for d in (1, 2, 3)]
    kv_own = lax.all_to_all(kv_pos, "y", 0, 0, tiled=True)
    near = {0: kv_own}
    for d in (1, 2, 3):
        near[d] = ring(kv_own, "x", d, 4)
    arrived = lax.all_to_all(
        upstream.reshape(128, 1, 1, 2048), ("z", "y", "x", "c"), split_axis=0, concat_axis=2, tiled=True
    )
    grad = arrived.reshape(B, 2048)
    far = {d: ring(near[d], "c", 1, 2) for d in range(4)}
    prev = [ring(k, SEQ, 1, 32) for k in cur]
    pay = call(payload, "payload", shape((4, PAY, HD), BF16), 0, 4)(
        grad, forward_out[0], queries[0], logsumexp[0]
    )
    pay_head = lax.all_to_all(pay, "y", 0, 0, tiled=True)
    part = {}
    mine, other, dq = make_own(2, True, False)(lengths, pay_head, near[2], far[2])
    part[2] = (mine, other)
    mine, other, dq = make_own(1, False, False)(lengths, pay_head, near[1], far[1], dq)
    part[1] = (mine, other)
    mine, other, dq = make_own(3, False, False)(lengths, pay_head, near[3], far[3], dq)
    part[3] = (mine, other)
    sib = call(
        sibling_kernel,
        "sibling",
        tuple([kv] * 6 + [shape((4, ROWS, HD), F32)]),
        2,
        7,
        [pltpu.VMEM((4, 2, ROWS), F32), pltpu.VMEM((HD, ROWS), F32)],
    )(lengths, sibling_mask.reshape(3), pay, *cur, *prev)
    mine, other, dq = make_own(0, False, True)(lengths, pay_head, near[0], far[0], dq)
    part[0] = (mine, other)
    back = {}
    for d in (2, 1, 3, 0):
        mine, other = part[d]
        both = mine.astype(F32) + ring(other, "c", 1, 2).astype(F32)
        back[d] = ring(both.astype(BF16), "x", -d, 4) if d else both
    own = back[0]
    for d in (1, 2, 3):
        own = own + back[d].astype(F32)
    dq_pos = lax.all_to_all(dq, "y", 0, 0, tiled=True)
    own_pos = lax.all_to_all(own.astype(BF16), "y", 0, 0, tiled=True)
    sums = []
    for d in (1, 2, 3):
        late = ring(sib[2 + d], SEQ, -1, 32).astype(F32)
        sums.append(ring((sib[d - 1].astype(F32) + late).astype(BF16), "z", -d, 4))
    row = shape((B, 512), BF16)
    out = call(finish, "finish", (shape((B, 2048), BF16), row, row), 0, 6)(
        dq_pos, sib[6], own_pos, *sums
    )
    return tuple(o[None] for o in out)


def solution(mesh):
    grid = Mesh(mesh.devices.reshape(4, 4, 4, 2), ("z",) + SEQ)
    rows = P("z", SEQ, None)
    return jax.shard_map(
        shards,
        mesh=grid,
        in_specs=(
            rows,
            rows,
            rows,
            rows,
            P("z", None, SEQ),
            P(None, ("z",) + SEQ, None),
            P(),
            P("z", None, SEQ),
        ),
        out_specs=(rows, rows, rows),
        check_vma=False,
    )
```

```python
import jax
import jax.numpy as jnp
from jax import lax
from jax.experimental import pallas as pl
from jax.experimental.pallas import tpu as pltpu
from jax.sharding import Mesh, PartitionSpec as P


B = 128
HD = 128
GROUP = 4
HEADS = 4
ROWS = GROUP * B
QO = 2 * ROWS + 16
FACTOR = HD**-0.5
LOG2E = 1.4426950408889634
SCALE = FACTOR * LOG2E
DEAD = 1e30
F32 = jnp.float32
BF16 = jnp.bfloat16
SEQ = ("y", "x", "c")
VMEM = pl.BlockSpec(memory_space=pltpu.VMEM)
SMEM = pl.BlockSpec(memory_space=pltpu.SMEM)


def nt(a, b):
    return lax.dot_general(a, b, (((1,), (1,)), ((), ())), preferred_element_type=F32)


def nn(a, b):
    return jnp.dot(a, b, preferred_element_type=F32)


def call(kernel, outs, n_smem, n_vmem, scratch=(), aliases=None):
    return pl.pallas_call(
        kernel,
        out_shape=outs,
        in_specs=[SMEM] * n_smem + [VMEM] * n_vmem,
        out_specs=jax.tree.map(lambda _: VMEM, outs),
        scratch_shapes=list(scratch),
        input_output_aliases=aliases or {},
        compiler_params=pltpu.CompilerParams(vmem_limit_bytes=48 << 20),
    )


def shape(dims, dtype):
    return jax.ShapeDtypeStruct(dims, dtype)


def prep_kv(k_ref, v_ref, *outs):
    y = lax.axis_index("y")
    for d in range(HEADS):
        cols = pl.ds(pl.multiple_of(lax.rem(y + d, 4) * HD, HD), HD)
        outs[d][0] = k_ref[:, cols]
        outs[d][1] = v_ref[:, cols]


def three(x):
    high = x.astype(BF16)
    rest = x - high.astype(F32)
    mid = rest.astype(BF16)
    low = (rest - mid.astype(F32)).astype(BF16)
    return [high.astype(F32), mid.astype(F32), low.astype(F32)]


def prep_qo(mask_ref, q_ref, o_ref, lse_ref, *outs):
    y = lax.axis_index("y")
    marks = [jnp.full((1, HD), mask_ref[n].astype(F32)) for n in range(3)] + [jnp.zeros((1, HD), F32)]
    for d in range(HEADS):
        head = lax.rem(y + d, 4)
        for g in range(GROUP):
            cols = pl.ds(pl.multiple_of((head * GROUP + g) * HD, HD), HD)
            outs[d][g * B : (g + 1) * B, :] = q_ref[:, cols]
            outs[d][ROWS + g * B : ROWS + (g + 1) * B, :] = o_ref[:, cols]
        outs[d][2 * ROWS : QO, :] = jnp.concatenate(three(lse_ref[head]) + marks, axis=0).astype(BF16)


def deal(up_ref, out_ref, wide_ref):
    for t in range(4):
        for c in range(4):
            for i in range(4):
                for g in range(GROUP):
                    cols = slice((c * GROUP + g) * HD, (c * GROUP + g + 1) * HD)
                    block = up_ref[(t * 4 + i) * 8 : (t * 4 + i + 1) * 8, cols]
                    wide_ref[(t * 4 + c) * 8 : (t * 4 + c + 1) * 8, i * GROUP + g, :] = block.astype(F32)
    out_ref[...] = wide_ref[...].astype(BF16)


def prepare(len_ref, g_ref, *refs):
    pieces, (p_ref, stat_ref, mark_ref, wide_ref) = refs[:4], refs[4:]
    y = lax.axis_index("y")
    length = len_ref[lax.axis_index("z")]
    shard = 2 * lax.axis_index("x") + lax.axis_index("c")
    lane = lax.broadcasted_iota(jnp.int32, (GROUP, B), 1)
    wide_ref[...] = g_ref[...].astype(F32)
    for n in range(16):
        p_ref[n // GROUP, ROWS + (n % GROUP) * B : ROWS + (n % GROUP + 1) * B, :] = wide_ref[:, n, :].astype(BF16)
    for d in range(4):
        i = lax.rem(y + 4 - d, 4)
        p_ref[i, 0:ROWS, :] = pieces[d][0:ROWS, :]
        raw = pieces[d][2 * ROWS : QO, :].astype(F32)
        lse = raw[0:4] + raw[4:8] + raw[8:12]
        lse = jnp.where((8 * i + shard) * B + lane < length, lse * LOG2E, DEAD)
        mark_ref[i] = raw[8:16]
        for g in range(GROUP):
            grad = p_ref[i, ROWS + g * B : ROWS + (g + 1) * B, :]
            out = pieces[d][ROWS + g * B : ROWS + (g + 1) * B, :]
            prod = grad.astype(F32) * out.astype(F32)
            stat_ref[i, 0:1, g * B : (g + 1) * B] = jnp.sum(prod.T, axis=0, keepdims=True)
            stat_ref[i, 1:2, g * B : (g + 1) * B] = lse[g : g + 1]


def weigh(keys, vals, p_ref, stat_ref, i, allow, prob_ref, ds_ref):
    q = p_ref[i, 0:ROWS, :]
    grad = p_ref[i, ROWS : 2 * ROWS, :]
    prob = jnp.exp2(nt(keys, q) * SCALE - stat_ref[i, 1:2, :])
    if allow is not None:
        prob = jnp.where(allow, prob, 0.0)
    diff = nt(vals, grad) - stat_ref[i, 0:1, :]
    prob_ref[...] = prob.astype(BF16)
    ds_ref[...] = (prob * diff).astype(BF16)


MS = sum(m << (2 * t) for t, m in enumerate((0, 0, 0, 1, 1, 2, 0, 1, 2, 3)))
QS = sum(i << (2 * t) for t, i in enumerate((1, 2, 3, 2, 3, 3, 0, 1, 2, 3)))


def make_own(dist, first, last):
    def kernel(p_ref, stat_ref, km_ref, ko_ref, *refs):
        if not first:
            dq_in, refs = refs[0], refs[1:]
        dm_ref, do_ref, refs = refs[0], refs[1], refs[2:]
        if last:
            dq_outs, refs = refs[:4], refs[4:]
            kt_ref, dk_ref, dv_ref, p0, s0, p1, s1, acc_ref = refs
        else:
            acc_ref, kt_ref, dk_ref, dv_ref, p0, s0, p1, s1 = refs
        chip = lax.axis_index("x")
        core = lax.axis_index("c")
        y = lax.axis_index("y")
        if first:
            acc_ref[...] = jnp.zeros_like(acc_ref)
        else:
            acc_ref[...] = dq_in[...]
        dk_ref[...] = jnp.zeros_like(dk_ref)
        dv_ref[...] = jnp.zeros_like(dv_ref)
        for m in range(4):
            kt_ref[m] = jnp.concatenate([km_ref[m, 0], ko_ref[m, 0]], axis=0).T
        if dist == 0:
            count = 10
        else:
            count = jnp.where(lax.rem(chip + 4 - dist, 4) < chip, 10, 6)

        def which(t):
            t = jnp.minimum(t, count - 1)
            m = lax.shift_right_logical(jnp.int32(MS), 2 * t) & 3
            i = lax.shift_right_logical(jnp.int32(QS), 2 * t) & 3
            return m, i, (y - m) & 3

        def before(t, prob_ref, ds_ref):
            m, i, slot = which(t)
            keys = jnp.concatenate([km_ref[slot, 0], ko_ref[slot, 0]], axis=0)
            vals = jnp.concatenate([km_ref[slot, 1], ko_ref[slot, 1]], axis=0)
            allow = None
            if dist == 0:
                row = lax.broadcasted_iota(jnp.int32, (2 * B, ROWS), 0)
                col = lax.broadcasted_iota(jnp.int32, (1, ROWS), 1)
                row = jnp.where(core == 0, row, row ^ B)
                allow = row <= core * B + col % B + jnp.where(i > m, 4 * B, 0)
            weigh(keys, vals, p_ref, stat_ref, i, allow, prob_ref, ds_ref)

        def after(t, prob_ref, ds_ref):
            _, i, slot = which(t)
            dv_ref[slot] += nn(prob_ref[...], p_ref[i, ROWS : 2 * ROWS, :])
            dk_ref[slot] += nn(ds_ref[...], p_ref[i, 0:ROWS, :])
            acc_ref[i] += nn(kt_ref[slot], ds_ref[...])

        before(0, p0, s0)

        def two(u, carry):
            before(2 * u + 1, p1, s1)
            after(2 * u, p0, s0)
            before(2 * u + 2, p0, s0)
            after(2 * u + 1, p1, s1)
            return carry

        lax.fori_loop(0, count // 2, two, 0)
        for m in range(4):
            dk = (dk_ref[m] * FACTOR).astype(BF16)
            dv = dv_ref[m].astype(BF16)
            dm_ref[m, 0] = dk[:B]
            dm_ref[m, 1] = dv[:B]
            do_ref[m, 0] = dk[B:]
            do_ref[m, 1] = dv[B:]
        if last:
            for d in range(4):
                dq_outs[d][...] = (acc_ref[(y - d) & 3].T * FACTOR).astype(BF16)

    kv = shape((4, 2, B, HD), BF16)
    dq = [shape((ROWS, HD), BF16)] * 4 if last else [shape((4, HD, ROWS), F32)]
    scratch = [
        pltpu.VMEM((4, HD, 2 * B), BF16),
        pltpu.VMEM((4, 2 * B, HD), F32),
        pltpu.VMEM((4, 2 * B, HD), F32),
    ] + [pltpu.VMEM((2 * B, ROWS), BF16)] * 4
    if last:
        scratch.append(pltpu.VMEM((4, HD, ROWS), F32))
    return call(kernel, (kv, kv, *dq), 0, 4 if first else 5, scratch)


def sibling_kernel(len_ref, p_ref, stat_ref, mark_ref, dq_in, *refs):
    cur, prev, refs = refs[0:3], refs[3:6], refs[6:]
    dcur, dprev, acc_ref, k_ref, v_ref, list_ref, p0, s0, p1, s1 = refs
    thinker = lax.axis_index("z")
    y = lax.axis_index("y")
    shard = 2 * lax.axis_index("x") + lax.axis_index("c")
    length = len_ref[thinker]
    acc_ref[...] = dq_in[...]
    dcur[...] = jnp.zeros_like(dcur)
    dprev[...] = jnp.zeros_like(dprev)
    step = (shard == 0).astype(jnp.int32)
    count = jnp.int32(0)
    for i in range(4):
        slot = (y - i) & 3
        old = (slot + step) & 3
        block = 8 * i + shard
        for n in range(3):
            code = i * 4 + n
            k_ref[code, :B] = prev[n][old, 0]
            k_ref[code, B:] = cur[n][slot, 0]
            v_ref[code, :B] = prev[n][old, 1]
            v_ref[code, B:] = cur[n][slot, 1]
            top = len_ref[(thinker - 1 - n) & 3] - (block - 1) * B
            wanted = jnp.max(mark_ref[i, 6 - n : 7 - n, :]) > 0.5
            list_ref[count] = code
            count = count + (wanted & (block * B < length) & (top > 0)).astype(jnp.int32)
    list_ref[count] = 0
    list_ref[count + 1] = 0
    list_ref[count + 2] = 0

    def before(t, prob_ref, ds_ref):
        code = list_ref[t]
        i, n = code // 4, code & 3
        block = 8 * i + shard
        top = len_ref[(thinker - 1 - n) & 3] - (block - 1) * B
        low = jnp.where(block == 0, B, 0)
        top = jnp.where(t < count, top, 0)
        row = lax.broadcasted_iota(jnp.int32, (2 * B, ROWS), 0)
        col = lax.broadcasted_iota(jnp.int32, (1, ROWS), 1) % B
        allow = (row > jnp.maximum(col, low - 1)) & (row <= jnp.minimum(col + B, top - 1))
        weigh(k_ref[code], v_ref[code], p_ref, stat_ref, i, allow, prob_ref, ds_ref)

    def after(t, prob_ref, ds_ref):
        code = list_ref[t]
        i, n = code // 4, code & 3
        slot = (y - i) & 3
        old = (slot + step) & 3
        dv = nn(prob_ref[...], p_ref[i, ROWS : 2 * ROWS, :])
        dk = nn(ds_ref[...], p_ref[i, 0:ROWS, :]) * FACTOR
        acc_ref[i] += nn(k_ref[code].T, ds_ref[...])
        for kind, grad in ((0, dk), (1, dv)):
            dprev[n, old, kind] = (dprev[n, old, kind].astype(F32) + grad[:B]).astype(BF16)
            dcur[n, slot, kind] = (dcur[n, slot, kind].astype(F32) + grad[B:]).astype(BF16)

    @pl.when(count > 0)
    def _():
        before(0, p0, s0)

        def two(u, carry):
            before(2 * u + 1, p1, s1)
            after(2 * u, p0, s0)
            before(2 * u + 2, p0, s0)
            after(2 * u + 1, p1, s1)
            return carry

        lax.fori_loop(0, (count + 1) // 2, two, 0)


def merge(cur_ref, late_ref, *outs):
    for n in range(3):
        outs[n][...] = (cur_ref[n].astype(F32) + late_ref[n].astype(F32)).astype(BF16)


def gather_terms(*refs):
    terms, outs = refs[:-4], refs[-4:]
    for slot in range(4):
        total = terms[0][slot].astype(F32)
        for term in terms[1:]:
            total = total + term[slot].astype(F32)
        outs[slot][...] = total.astype(BF16)


def finish_q(d0, d1, d2, d3, out):
    y = lax.axis_index("y")
    for d, ref in enumerate((d0, d1, d2, d3)):
        head = lax.rem(y + d, 4)
        for g in range(GROUP):
            cols = pl.ds(pl.multiple_of((head * GROUP + g) * HD, HD), HD)
            out[:, cols] = ref[g * B : (g + 1) * B, :]


def finish_kv(d0, d1, d2, d3, k_out, v_out):
    y = lax.axis_index("y")
    for d, ref in enumerate((d0, d1, d2, d3)):
        cols = pl.ds(pl.multiple_of(lax.rem(y + d, 4) * HD, HD), HD)
        k_out[:, cols] = ref[0]
        v_out[:, cols] = ref[1]


def ring(x, axis, step, count):
    return lax.ppermute(x, axis, [(j, (j + step) % count) for j in range(count)])


def step(queries, keys, values, forward_out, logsumexp, upstream, lengths, sibling_mask):
    kv = shape((4, 2, B, HD), BF16)
    piece = shape((2, B, HD), BF16)
    row = shape((B, 512), BF16)
    core = ("x", "c")
    dists = (1, 2, 3)
    kv_sent = call(prep_kv, (piece,) * 4, 0, 2)(keys[0], values[0])
    kv_own = jnp.stack([kv_sent[0]] + [ring(kv_sent[d], "y", d, 4) for d in dists])
    qo_sent = call(prep_qo, (shape((QO, HD), BF16),) * 4, 1, 3)(
        sibling_mask.reshape(3), queries[0], forward_out[0], logsumexp.reshape(4, GROUP, B)
    )
    qo = [qo_sent[0]] + [ring(qo_sent[d], "y", d, 4) for d in dists]
    near = [kv_own] + [ring(kv_own, "x", d, 4) for d in dists]
    cur = [ring(kv_own, "z", d, 4) for d in dists]
    dealt = call(deal, shape((128, 16, HD), BF16), 0, 1, [pltpu.VMEM((128, 16, HD), F32)])(
        upstream.reshape(128, 2048)
    )
    arrived = lax.all_to_all(dealt, ("z", "y", "x", "c"), 0, 0, tiled=True)
    far = [ring(near[d], "c", 1, 2) for d in range(4)]
    prev = [ring(k, core, 1, 8) for k in cur]
    pay, stat, mark = call(
        prepare,
        (shape((4, 2 * ROWS, HD), BF16), shape((4, 2, ROWS), F32), shape((4, 8, HD), F32)),
        1,
        5,
        [pltpu.VMEM((128, 16, HD), F32)],
    )(lengths, arrived, *qo)
    mine, other, dq = {}, {}, None
    mine[2], other[2], dq = make_own(2, True, False)(pay, stat, near[2], far[2])
    trio = shape((3, 4, 2, B, HD), BF16)
    scratch = [pltpu.VMEM((16, 2 * B, HD), BF16)] * 2 + [pltpu.SMEM((16,), jnp.int32)]
    scratch += [pltpu.VMEM((2 * B, ROWS), BF16)] * 4
    sibling = call(sibling_kernel, (trio, trio, shape((4, HD, ROWS), F32)), 1, 10, scratch)
    dcur, dprev, dq = sibling(lengths, pay, stat, mark, dq, *cur, *prev)
    mine[3], other[3], dq = make_own(3, False, False)(pay, stat, near[3], far[3], dq)
    mine[1], other[1], dq = make_own(1, False, False)(pay, stat, near[1], far[1], dq)
    mine[0], other[0], *dq_sent = make_own(0, False, True)(pay, stat, near[0], far[0], dq)
    terms = [mine[0], ring(other[0], "c", 1, 2)]
    for d in (2, 1, 3):
        both = mine[d].astype(F32) + ring(other[d], "c", 1, 2).astype(F32)
        terms.append(ring(both.astype(BF16), "x", -d, 4))
    late = ring(dprev, core, -1, 8)
    merged = call(merge, (kv,) * 3, 0, 2)(dcur, late)
    terms += [ring(merged[d - 1], "z", -d, 4) for d in dists]
    dq_got = [dq_sent[0]] + [ring(dq_sent[d], "y", -d, 4) for d in dists]
    q_grad = call(finish_q, (shape((B, 2048), BF16),), 0, 4)(*dq_got)[0]
    kv_out = call(gather_terms, (piece,) * 4, 0, 8)(*terms)
    kv_got = [kv_out[0]] + [ring(kv_out[d], "y", -d, 4) for d in dists]
    k_grad, v_grad = call(finish_kv, (row, row), 0, 4)(*kv_got)
    return q_grad[None], k_grad[None], v_grad[None]


def solution(mesh):
    grid = Mesh(mesh.devices.reshape(4, 4, 4, 2), ("z",) + SEQ)
    rows = P("z", SEQ, None)
    return jax.shard_map(
        step,
        mesh=grid,
        in_specs=(
            rows,
            rows,
            rows,
            rows,
            P("z", None, SEQ),
            P(None, ("z",) + SEQ, None),
            P(),
            P("z", None, SEQ),
        ),
        out_specs=(rows, rows, rows),
        check_vma=False,
    )
```

```python
import jax
import jax.numpy as jnp
from jax import lax
from jax.experimental import pallas as pl
from jax.experimental.pallas import tpu as pltpu
from jax.sharding import Mesh, PartitionSpec as P


B = 128
HD = 128
GROUP = 4
HEADS = 4
ROWS = GROUP * B
QO = 2 * ROWS + 16
FACTOR = HD**-0.5
LOG2E = 1.4426950408889634
SCALE = FACTOR * LOG2E
DEAD = 1e30
F32 = jnp.float32
BF16 = jnp.bfloat16
SEQ = ("y", "x", "c")
VMEM = pl.BlockSpec(memory_space=pltpu.VMEM)
SMEM = pl.BlockSpec(memory_space=pltpu.SMEM)


def nt(a, b):
    return lax.dot_general(a, b, (((1,), (1,)), ((), ())), preferred_element_type=F32)


def nn(a, b):
    return jnp.dot(a, b, preferred_element_type=F32)


def call(kernel, outs, n_smem, n_vmem, scratch=(), aliases=None):
    return pl.pallas_call(
        kernel,
        out_shape=outs,
        in_specs=[SMEM] * n_smem + [VMEM] * n_vmem,
        out_specs=jax.tree.map(lambda _: VMEM, outs),
        scratch_shapes=list(scratch),
        input_output_aliases=aliases or {},
        compiler_params=pltpu.CompilerParams(vmem_limit_bytes=48 << 20),
    )


def shape(dims, dtype):
    return jax.ShapeDtypeStruct(dims, dtype)


def prep_kv(k_ref, v_ref, *outs):
    y = lax.axis_index("y")
    for d in range(HEADS):
        cols = pl.ds(pl.multiple_of(lax.rem(y + d, 4) * HD, HD), HD)
        outs[d][0] = k_ref[:, cols]
        outs[d][1] = v_ref[:, cols]


def three(x):
    high = x.astype(BF16)
    rest = x - high.astype(F32)
    mid = rest.astype(BF16)
    low = (rest - mid.astype(F32)).astype(BF16)
    return [high.astype(F32), mid.astype(F32), low.astype(F32)]


def prep_qo(mask_ref, q_ref, o_ref, lse_ref, *outs):
    y = lax.axis_index("y")
    marks = [jnp.full((1, HD), mask_ref[n].astype(F32)) for n in range(3)] + [jnp.zeros((1, HD), F32)]
    for d in range(HEADS):
        head = lax.rem(y + d, 4)
        for g in range(GROUP):
            cols = pl.ds(pl.multiple_of((head * GROUP + g) * HD, HD), HD)
            outs[d][g * B : (g + 1) * B, :] = q_ref[:, cols]
            outs[d][ROWS + g * B : ROWS + (g + 1) * B, :] = o_ref[:, cols]
        outs[d][2 * ROWS : QO, :] = jnp.concatenate(three(lse_ref[head]) + marks, axis=0).astype(BF16)


def deal(up_ref, out_ref, wide_ref):
    for t in range(4):
        for c in range(4):
            for i in range(4):
                for g in range(GROUP):
                    cols = slice((c * GROUP + g) * HD, (c * GROUP + g + 1) * HD)
                    block = up_ref[(t * 4 + i) * 8 : (t * 4 + i + 1) * 8, cols]
                    wide_ref[(t * 4 + c) * 8 : (t * 4 + c + 1) * 8, i * GROUP + g, :] = block.astype(F32)
    out_ref[...] = wide_ref[...].astype(BF16)


def prepare(len_ref, g_ref, *refs):
    pieces, (p_ref, stat_ref, mark_ref, wide_ref) = refs[:4], refs[4:]
    y = lax.axis_index("y")
    length = len_ref[lax.axis_index("z")]
    shard = 2 * lax.axis_index("x") + lax.axis_index("c")
    lane = lax.broadcasted_iota(jnp.int32, (GROUP, B), 1)
    wide_ref[...] = g_ref[...].astype(F32)
    for n in range(16):
        p_ref[n // GROUP, ROWS + (n % GROUP) * B : ROWS + (n % GROUP + 1) * B, :] = wide_ref[:, n, :].astype(BF16)
    for d in range(4):
        i = lax.rem(y + 4 - d, 4)
        p_ref[i, 0:ROWS, :] = pieces[d][0:ROWS, :]
        raw = pieces[d][2 * ROWS : QO, :].astype(F32)
        lse = raw[0:4] + raw[4:8] + raw[8:12]
        lse = jnp.where((8 * i + shard) * B + lane < length, lse * LOG2E, DEAD)
        mark_ref[i] = raw[8:16]
        for g in range(GROUP):
            grad = p_ref[i, ROWS + g * B : ROWS + (g + 1) * B, :]
            out = pieces[d][ROWS + g * B : ROWS + (g + 1) * B, :]
            prod = grad.astype(F32) * out.astype(F32)
            stat_ref[i, 0:1, g * B : (g + 1) * B] = jnp.sum(prod.T, axis=0, keepdims=True)
            stat_ref[i, 1:2, g * B : (g + 1) * B] = lse[g : g + 1]


def weigh(keys, vals, p_ref, stat_ref, i, allow, prob_ref, ds_ref):
    q = p_ref[i, 0:ROWS, :]
    grad = p_ref[i, ROWS : 2 * ROWS, :]
    prob = jnp.exp2(nt(keys, q) * SCALE - stat_ref[i, 1:2, :])
    if allow is not None:
        prob = jnp.where(allow, prob, 0.0)
    diff = nt(vals, grad) - stat_ref[i, 0:1, :]
    prob_ref[...] = prob.astype(BF16)
    ds_ref[...] = (prob * diff).astype(BF16)


MS = sum(m << (2 * t) for t, m in enumerate((0, 0, 0, 1, 1, 2, 0, 1, 2, 3)))
QS = sum(i << (2 * t) for t, i in enumerate((1, 2, 3, 2, 3, 3, 0, 1, 2, 3)))


def make_own(dist, first, last):
    def kernel(p_ref, stat_ref, km_ref, ko_ref, *refs):
        if not first:
            dq_in, refs = refs[0], refs[1:]
        dm_ref, do_ref, refs = refs[0], refs[1], refs[2:]
        if last:
            dq_outs, refs = refs[:4], refs[4:]
            kt_ref, dk_ref, dv_ref, p0, s0, p1, s1, acc_ref = refs
        else:
            acc_ref, kt_ref, dk_ref, dv_ref, p0, s0, p1, s1 = refs
        chip = lax.axis_index("x")
        core = lax.axis_index("c")
        y = lax.axis_index("y")
        if first:
            acc_ref[...] = jnp.zeros_like(acc_ref)
        else:
            acc_ref[...] = dq_in[...]
        dk_ref[...] = jnp.zeros_like(dk_ref)
        dv_ref[...] = jnp.zeros_like(dv_ref)
        for m in range(4):
            kt_ref[m] = jnp.concatenate([km_ref[m, 0], ko_ref[m, 0]], axis=0).T
        if dist == 0:
            count = 10
        else:
            count = jnp.where(lax.rem(chip + 4 - dist, 4) < chip, 10, 6)

        def which(t):
            t = jnp.minimum(t, count - 1)
            m = lax.shift_right_logical(jnp.int32(MS), 2 * t) & 3
            i = lax.shift_right_logical(jnp.int32(QS), 2 * t) & 3
            return m, i, (y - m) & 3

        def before(t, prob_ref, ds_ref):
            m, i, slot = which(t)
            keys = jnp.concatenate([km_ref[slot, 0], ko_ref[slot, 0]], axis=0)
            vals = jnp.concatenate([km_ref[slot, 1], ko_ref[slot, 1]], axis=0)
            allow = None
            if dist == 0:
                row = lax.broadcasted_iota(jnp.int32, (2 * B, ROWS), 0)
                col = lax.broadcasted_iota(jnp.int32, (1, ROWS), 1)
                row = jnp.where(core == 0, row, row ^ B)
                allow = row <= core * B + col % B + jnp.where(i > m, 4 * B, 0)
            weigh(keys, vals, p_ref, stat_ref, i, allow, prob_ref, ds_ref)

        def after(t, prob_ref, ds_ref):
            _, i, slot = which(t)
            dv_ref[slot] += nn(prob_ref[...], p_ref[i, ROWS : 2 * ROWS, :])
            dk_ref[slot] += nn(ds_ref[...], p_ref[i, 0:ROWS, :])
            acc_ref[i] += nn(kt_ref[slot], ds_ref[...])

        before(0, p0, s0)

        def two(u, carry):
            before(2 * u + 1, p1, s1)
            after(2 * u, p0, s0)
            before(2 * u + 2, p0, s0)
            after(2 * u + 1, p1, s1)
            return carry

        lax.fori_loop(0, count // 2, two, 0)
        for m in range(4):
            dk = (dk_ref[m] * FACTOR).astype(BF16)
            dv = dv_ref[m].astype(BF16)
            dm_ref[m, 0] = dk[:B]
            dm_ref[m, 1] = dv[:B]
            do_ref[m, 0] = dk[B:]
            do_ref[m, 1] = dv[B:]
        if last:
            for d in range(4):
                dq_outs[d][...] = (acc_ref[(y - d) & 3].T * FACTOR).astype(BF16)

    kv = shape((4, 2, B, HD), BF16)
    dq = [shape((ROWS, HD), BF16)] * 4 if last else [shape((4, HD, ROWS), F32)]
    scratch = [
        pltpu.VMEM((4, HD, 2 * B), BF16),
        pltpu.VMEM((4, 2 * B, HD), F32),
        pltpu.VMEM((4, 2 * B, HD), F32),
    ] + [pltpu.VMEM((2 * B, ROWS), BF16)] * 4
    if last:
        scratch.append(pltpu.VMEM((4, HD, ROWS), F32))
    return call(kernel, (kv, kv, *dq), 0, 4 if first else 5, scratch)


def sibling_kernel(len_ref, p_ref, stat_ref, mark_ref, dq_in, *refs):
    cur, prev, refs = refs[0:3], refs[3:6], refs[6:]
    dcur, dprev, acc_ref, k_ref, v_ref, list_ref, p0, s0, p1, s1 = refs
    thinker = lax.axis_index("z")
    y = lax.axis_index("y")
    shard = 2 * lax.axis_index("x") + lax.axis_index("c")
    length = len_ref[thinker]
    acc_ref[...] = dq_in[...]
    dcur[...] = jnp.zeros_like(dcur)
    dprev[...] = jnp.zeros_like(dprev)
    step = (shard == 0).astype(jnp.int32)
    count = jnp.int32(0)
    for i in range(4):
        slot = (y - i) & 3
        old = (slot + step) & 3
        block = 8 * i + shard
        for n in range(3):
            code = i * 4 + n
            k_ref[code, :B] = prev[n][old, 0]
            k_ref[code, B:] = cur[n][slot, 0]
            v_ref[code, :B] = prev[n][old, 1]
            v_ref[code, B:] = cur[n][slot, 1]
            top = len_ref[(thinker - 1 - n) & 3] - (block - 1) * B
            wanted = jnp.max(mark_ref[i, 6 - n : 7 - n, :]) > 0.5
            list_ref[count] = code
            count = count + (wanted & (block * B < length) & (top > 0)).astype(jnp.int32)
    list_ref[count] = 0
    list_ref[count + 1] = 0
    list_ref[count + 2] = 0

    def before(t, prob_ref, ds_ref):
        code = list_ref[t]
        i, n = code // 4, code & 3
        block = 8 * i + shard
        top = len_ref[(thinker - 1 - n) & 3] - (block - 1) * B
        low = jnp.where(block == 0, B, 0)
        top = jnp.where(t < count, top, 0)
        row = lax.broadcasted_iota(jnp.int32, (2 * B, ROWS), 0)
        col = lax.broadcasted_iota(jnp.int32, (1, ROWS), 1) % B
        allow = (row > jnp.maximum(col, low - 1)) & (row <= jnp.minimum(col + B, top - 1))
        weigh(k_ref[code], v_ref[code], p_ref, stat_ref, i, allow, prob_ref, ds_ref)

    def after(t, prob_ref, ds_ref):
        code = list_ref[t]
        i, n = code // 4, code & 3
        slot = (y - i) & 3
        old = (slot + step) & 3
        dv = nn(prob_ref[...], p_ref[i, ROWS : 2 * ROWS, :])
        dk = nn(ds_ref[...], p_ref[i, 0:ROWS, :]) * FACTOR
        acc_ref[i] += nn(k_ref[code].T, ds_ref[...])
        for kind, grad in ((0, dk), (1, dv)):
            dprev[n, old, kind] = (dprev[n, old, kind].astype(F32) + grad[:B]).astype(BF16)
            dcur[n, slot, kind] = (dcur[n, slot, kind].astype(F32) + grad[B:]).astype(BF16)

    @pl.when(count > 0)
    def _():
        before(0, p0, s0)

        def two(u, carry):
            before(2 * u + 1, p1, s1)
            after(2 * u, p0, s0)
            before(2 * u + 2, p0, s0)
            after(2 * u + 1, p1, s1)
            return carry

        lax.fori_loop(0, (count + 1) // 2, two, 0)


def merge(cur_ref, late_ref, *outs):
    for n in range(3):
        outs[n][...] = (cur_ref[n].astype(F32) + late_ref[n].astype(F32)).astype(BF16)


def gather_terms(*refs):
    terms, outs = refs[:-4], refs[-4:]
    for slot in range(4):
        total = terms[0][slot].astype(F32)
        for term in terms[1:]:
            total = total + term[slot].astype(F32)
        outs[slot][...] = total.astype(BF16)


def finish_q(d0, d1, d2, d3, out):
    y = lax.axis_index("y")
    for d, ref in enumerate((d0, d1, d2, d3)):
        head = lax.rem(y + d, 4)
        for g in range(GROUP):
            cols = pl.ds(pl.multiple_of((head * GROUP + g) * HD, HD), HD)
            out[:, cols] = ref[g * B : (g + 1) * B, :]


def finish_kv(d0, d1, d2, d3, k_out, v_out):
    y = lax.axis_index("y")
    for d, ref in enumerate((d0, d1, d2, d3)):
        cols = pl.ds(pl.multiple_of(lax.rem(y + d, 4) * HD, HD), HD)
        k_out[:, cols] = ref[0]
        v_out[:, cols] = ref[1]


def ring(x, axis, step, count):
    return lax.ppermute(x, axis, [(j, (j + step) % count) for j in range(count)])


def step(queries, keys, values, forward_out, logsumexp, upstream, lengths, sibling_mask):
    kv = shape((4, 2, B, HD), BF16)
    piece = shape((2, B, HD), BF16)
    row = shape((B, 512), BF16)
    core = ("x", "c")
    dists = (1, 2, 3)
    kv_sent = call(prep_kv, (piece,) * 4, 0, 2)(keys[0], values[0])
    kv_own = jnp.stack([kv_sent[0]] + [ring(kv_sent[d], "y", d, 4) for d in dists])
    qo_sent = call(prep_qo, (shape((QO, HD), BF16),) * 4, 1, 3)(
        sibling_mask.reshape(3), queries[0], forward_out[0], logsumexp.reshape(4, GROUP, B)
    )
    qo = [qo_sent[0]] + [ring(qo_sent[d], "y", d, 4) for d in dists]
    near = [kv_own] + [ring(kv_own, "x", d, 4) for d in dists]
    cur = [ring(kv_own, "z", d, 4) for d in dists]
    dealt = call(deal, shape((128, 16, HD), BF16), 0, 1, [pltpu.VMEM((128, 16, HD), F32)])(
        upstream.reshape(128, 2048)
    )
    arrived = lax.all_to_all(dealt, ("z", "y", "x", "c"), 0, 0, tiled=True)
    far = [ring(near[d], "c", 1, 2) for d in range(4)]
    prev = [ring(k, core, 1, 8) for k in cur]
    pay, stat, mark = call(
        prepare,
        (shape((4, 2 * ROWS, HD), BF16), shape((4, 2, ROWS), F32), shape((4, 8, HD), F32)),
        1,
        5,
        [pltpu.VMEM((128, 16, HD), F32)],
    )(lengths, arrived, *qo)
    mine, other, dq = {}, {}, None
    mine[0], other[0], dq = make_own(0, True, False)(pay, stat, near[0], far[0])
    mine[2], other[2], dq = make_own(2, False, False)(pay, stat, near[2], far[2], dq)
    trio = shape((3, 4, 2, B, HD), BF16)
    scratch = [pltpu.VMEM((16, 2 * B, HD), BF16)] * 2 + [pltpu.SMEM((16,), jnp.int32)]
    scratch += [pltpu.VMEM((2 * B, ROWS), BF16)] * 4
    sibling = call(sibling_kernel, (trio, trio, shape((4, HD, ROWS), F32)), 1, 10, scratch)
    dcur, dprev, dq = sibling(lengths, pay, stat, mark, dq, *cur, *prev)
    mine[3], other[3], dq = make_own(3, False, False)(pay, stat, near[3], far[3], dq)
    mine[1], other[1], *dq_sent = make_own(1, False, True)(pay, stat, near[1], far[1], dq)
    terms = [mine[0], ring(other[0], "c", 1, 2)]
    for d in (2, 1, 3):
        both = mine[d].astype(F32) + ring(other[d], "c", 1, 2).astype(F32)
        terms.append(ring(both.astype(BF16), "x", -d, 4))
    late = ring(dprev, core, -1, 8)
    merged = call(merge, (kv,) * 3, 0, 2)(dcur, late)
    terms += [ring(merged[d - 1], "z", -d, 4) for d in dists]
    dq_got = [dq_sent[0]] + [ring(dq_sent[d], "y", -d, 4) for d in dists]
    q_grad = call(finish_q, (shape((B, 2048), BF16),), 0, 4)(*dq_got)[0]
    kv_out = call(gather_terms, (piece,) * 4, 0, 8)(*terms)
    kv_got = [kv_out[0]] + [ring(kv_out[d], "y", -d, 4) for d in dists]
    k_grad, v_grad = call(finish_kv, (row, row), 0, 4)(*kv_got)
    return q_grad[None], k_grad[None], v_grad[None]


def solution(mesh):
    grid = Mesh(mesh.devices.reshape(4, 4, 4, 2), ("z",) + SEQ)
    rows = P("z", SEQ, None)
    return jax.shard_map(
        step,
        mesh=grid,
        in_specs=(
            rows,
            rows,
            rows,
            rows,
            P("z", None, SEQ),
            P(None, ("z",) + SEQ, None),
            P(),
            P("z", None, SEQ),
        ),
        out_specs=(rows, rows, rows),
        check_vma=False,
    )
```

```python
import jax
import jax.numpy as jnp
from jax import lax
from jax.experimental import pallas as pl
from jax.experimental.pallas import tpu as pltpu
from jax.sharding import Mesh, PartitionSpec as P


B = 128
HD = 128
GROUP = 4
HEADS = 4
ROWS = GROUP * B
QO = 2 * ROWS + 16
FACTOR = HD**-0.5
LOG2E = 1.4426950408889634
SCALE = FACTOR * LOG2E
DEAD = 1e30
F32 = jnp.float32
BF16 = jnp.bfloat16
SEQ = ("y", "x", "c")
VMEM = pl.BlockSpec(memory_space=pltpu.VMEM)
SMEM = pl.BlockSpec(memory_space=pltpu.SMEM)


def nt(a, b):
    return lax.dot_general(a, b, (((1,), (1,)), ((), ())), preferred_element_type=F32)


def nn(a, b):
    return jnp.dot(a, b, preferred_element_type=F32)


def call(kernel, outs, n_smem, n_vmem, scratch=(), aliases=None):
    return pl.pallas_call(
        kernel,
        out_shape=outs,
        in_specs=[SMEM] * n_smem + [VMEM] * n_vmem,
        out_specs=jax.tree.map(lambda _: VMEM, outs),
        scratch_shapes=list(scratch),
        input_output_aliases=aliases or {},
        compiler_params=pltpu.CompilerParams(vmem_limit_bytes=48 << 20),
    )


def shape(dims, dtype):
    return jax.ShapeDtypeStruct(dims, dtype)


def prep_kv(k_ref, v_ref, *outs):
    y = lax.axis_index("y")
    for d in range(HEADS):
        cols = pl.ds(pl.multiple_of(lax.rem(y + d, 4) * HD, HD), HD)
        outs[d][0] = k_ref[:, cols]
        outs[d][1] = v_ref[:, cols]


def three(x):
    high = x.astype(BF16)
    rest = x - high.astype(F32)
    mid = rest.astype(BF16)
    low = (rest - mid.astype(F32)).astype(BF16)
    return [high.astype(F32), mid.astype(F32), low.astype(F32)]


def prep_qo(mask_ref, q_ref, o_ref, lse_ref, *outs):
    y = lax.axis_index("y")
    marks = [jnp.full((1, HD), mask_ref[n].astype(F32)) for n in range(3)] + [jnp.zeros((1, HD), F32)]
    for d in range(HEADS):
        head = lax.rem(y + d, 4)
        for g in range(GROUP):
            cols = pl.ds(pl.multiple_of((head * GROUP + g) * HD, HD), HD)
            outs[d][g * B : (g + 1) * B, :] = q_ref[:, cols]
            outs[d][ROWS + g * B : ROWS + (g + 1) * B, :] = o_ref[:, cols]
        outs[d][2 * ROWS : QO, :] = jnp.concatenate(three(lse_ref[head]) + marks, axis=0).astype(BF16)


def deal(up_ref, out_ref, wide_ref):
    for t in range(4):
        for c in range(4):
            for i in range(4):
                for g in range(GROUP):
                    cols = slice((c * GROUP + g) * HD, (c * GROUP + g + 1) * HD)
                    block = up_ref[(t * 4 + i) * 8 : (t * 4 + i + 1) * 8, cols]
                    wide_ref[(t * 4 + c) * 8 : (t * 4 + c + 1) * 8, i * GROUP + g, :] = block.astype(F32)
    out_ref[...] = wide_ref[...].astype(BF16)


def prepare(len_ref, g_ref, *refs):
    pieces, (p_ref, stat_ref, mark_ref, wide_ref) = refs[:4], refs[4:]
    y = lax.axis_index("y")
    length = len_ref[lax.axis_index("z")]
    shard = 2 * lax.axis_index("x") + lax.axis_index("c")
    lane = lax.broadcasted_iota(jnp.int32, (GROUP, B), 1)
    wide_ref[...] = g_ref[...].astype(F32)
    for n in range(16):
        p_ref[n // GROUP, ROWS + (n % GROUP) * B : ROWS + (n % GROUP + 1) * B, :] = wide_ref[:, n, :].astype(BF16)
    for d in range(4):
        i = lax.rem(y + 4 - d, 4)
        p_ref[i, 0:ROWS, :] = pieces[d][0:ROWS, :]
        raw = pieces[d][2 * ROWS : QO, :].astype(F32)
        lse = raw[0:4] + raw[4:8] + raw[8:12]
        lse = jnp.where((8 * i + shard) * B + lane < length, lse * LOG2E, DEAD)
        mark_ref[i] = raw[8:16]
        for g in range(GROUP):
            grad = p_ref[i, ROWS + g * B : ROWS + (g + 1) * B, :]
            out = pieces[d][ROWS + g * B : ROWS + (g + 1) * B, :]
            prod = grad.astype(F32) * out.astype(F32)
            stat_ref[i, 0:1, g * B : (g + 1) * B] = jnp.sum(prod.T, axis=0, keepdims=True)
            stat_ref[i, 1:2, g * B : (g + 1) * B] = lse[g : g + 1]


def weigh(keys, vals, p_ref, stat_ref, i, allow, prob_ref, ds_ref):
    q = p_ref[i, 0:ROWS, :]
    grad = p_ref[i, ROWS : 2 * ROWS, :]
    prob = jnp.exp2(nt(keys, q) * SCALE - stat_ref[i, 1:2, :])
    if allow is not None:
        prob = jnp.where(allow, prob, 0.0)
    diff = nt(vals, grad) - stat_ref[i, 0:1, :]
    prob_ref[...] = prob.astype(BF16)
    ds_ref[...] = (prob * diff).astype(BF16)


MS = sum(m << (2 * t) for t, m in enumerate((0, 0, 0, 1, 1, 2, 0, 1, 2, 3)))
QS = sum(i << (2 * t) for t, i in enumerate((1, 2, 3, 2, 3, 3, 0, 1, 2, 3)))


def make_own(dist, first, last):
    def kernel(p_ref, stat_ref, km_ref, ko_ref, *refs):
        if not first:
            dq_in, refs = refs[0], refs[1:]
        dm_ref, do_ref, refs = refs[0], refs[1], refs[2:]
        if last:
            dq_outs, refs = refs[:4], refs[4:]
            kt_ref, dk_ref, dv_ref, p0, s0, p1, s1, acc_ref = refs
        else:
            acc_ref, kt_ref, dk_ref, dv_ref, p0, s0, p1, s1 = refs
        chip = lax.axis_index("x")
        core = lax.axis_index("c")
        y = lax.axis_index("y")
        if first:
            acc_ref[...] = jnp.zeros_like(acc_ref)
        elif last:
            acc_ref[...] = dq_in[...]
        dk_ref[...] = jnp.zeros_like(dk_ref)
        dv_ref[...] = jnp.zeros_like(dv_ref)
        for m in range(4):
            kt_ref[m] = jnp.concatenate([km_ref[m, 0], ko_ref[m, 0]], axis=0).T
        if dist == 0:
            count = 10
        else:
            count = jnp.where(lax.rem(chip + 4 - dist, 4) < chip, 10, 6)

        def which(t):
            t = jnp.minimum(t, count - 1)
            m = lax.shift_right_logical(jnp.int32(MS), 2 * t) & 3
            i = lax.shift_right_logical(jnp.int32(QS), 2 * t) & 3
            return m, i, (y - m) & 3

        def before(t, prob_ref, ds_ref):
            m, i, slot = which(t)
            keys = jnp.concatenate([km_ref[slot, 0], ko_ref[slot, 0]], axis=0)
            vals = jnp.concatenate([km_ref[slot, 1], ko_ref[slot, 1]], axis=0)
            allow = None
            if dist == 0:
                row = lax.broadcasted_iota(jnp.int32, (2 * B, ROWS), 0)
                col = lax.broadcasted_iota(jnp.int32, (1, ROWS), 1)
                row = jnp.where(core == 0, row, row ^ B)
                allow = row <= core * B + col % B + jnp.where(i > m, 4 * B, 0)
            weigh(keys, vals, p_ref, stat_ref, i, allow, prob_ref, ds_ref)

        def after(t, prob_ref, ds_ref):
            _, i, slot = which(t)
            dv_ref[slot] += nn(prob_ref[...], p_ref[i, ROWS : 2 * ROWS, :])
            dk_ref[slot] += nn(ds_ref[...], p_ref[i, 0:ROWS, :])
            acc_ref[i] += nn(kt_ref[slot], ds_ref[...])

        before(0, p0, s0)

        def two(u, carry):
            before(2 * u + 1, p1, s1)
            after(2 * u, p0, s0)
            before(2 * u + 2, p0, s0)
            after(2 * u + 1, p1, s1)
            return carry

        lax.fori_loop(0, count // 2, two, 0)
        for m in range(4):
            dk = (dk_ref[m] * FACTOR).astype(BF16)
            dv = dv_ref[m].astype(BF16)
            dm_ref[m, 0] = dk[:B]
            dm_ref[m, 1] = dv[:B]
            do_ref[m, 0] = dk[B:]
            do_ref[m, 1] = dv[B:]
        if last:
            for d in range(4):
                dq_outs[d][...] = (acc_ref[(y - d) & 3].T * FACTOR).astype(BF16)

    kv = shape((4, 2, B, HD), BF16)
    dq = [shape((ROWS, HD), BF16)] * 4 if last else [shape((4, HD, ROWS), F32)]
    scratch = [
        pltpu.VMEM((4, HD, 2 * B), BF16),
        pltpu.VMEM((4, 2 * B, HD), F32),
        pltpu.VMEM((4, 2 * B, HD), F32),
    ] + [pltpu.VMEM((2 * B, ROWS), BF16)] * 4
    if last:
        scratch.append(pltpu.VMEM((4, HD, ROWS), F32))
    aliases = None if first or last else {4: 2}
    return call(kernel, (kv, kv, *dq), 0, 4 if first else 5, scratch, aliases)


def sibling_kernel(len_ref, p_ref, stat_ref, mark_ref, dq_in, *refs):
    cur, prev, refs = refs[0:3], refs[3:6], refs[6:]
    dcur, dprev, acc_ref, k_ref, v_ref, list_ref, p0, s0, p1, s1 = refs
    thinker = lax.axis_index("z")
    y = lax.axis_index("y")
    shard = 2 * lax.axis_index("x") + lax.axis_index("c")
    length = len_ref[thinker]
    del dq_in
    dcur[...] = jnp.zeros_like(dcur)
    dprev[...] = jnp.zeros_like(dprev)
    step = (shard == 0).astype(jnp.int32)
    count = jnp.int32(0)
    for i in range(4):
        slot = (y - i) & 3
        old = (slot + step) & 3
        block = 8 * i + shard
        for n in range(3):
            code = i * 4 + n
            k_ref[code, :B] = prev[n][old, 0]
            k_ref[code, B:] = cur[n][slot, 0]
            v_ref[code, :B] = prev[n][old, 1]
            v_ref[code, B:] = cur[n][slot, 1]
            top = len_ref[(thinker - 1 - n) & 3] - (block - 1) * B
            wanted = jnp.max(mark_ref[i, 6 - n : 7 - n, :]) > 0.5
            list_ref[count] = code
            count = count + (wanted & (block * B < length) & (top > 0)).astype(jnp.int32)
    list_ref[count] = 0
    list_ref[count + 1] = 0
    list_ref[count + 2] = 0

    def before(t, prob_ref, ds_ref):
        code = list_ref[t]
        i, n = code // 4, code & 3
        block = 8 * i + shard
        top = len_ref[(thinker - 1 - n) & 3] - (block - 1) * B
        low = jnp.where(block == 0, B, 0)
        top = jnp.where(t < count, top, 0)
        row = lax.broadcasted_iota(jnp.int32, (2 * B, ROWS), 0)
        col = lax.broadcasted_iota(jnp.int32, (1, ROWS), 1) % B
        allow = (row > jnp.maximum(col, low - 1)) & (row <= jnp.minimum(col + B, top - 1))
        weigh(k_ref[code], v_ref[code], p_ref, stat_ref, i, allow, prob_ref, ds_ref)

    def after(t, prob_ref, ds_ref):
        code = list_ref[t]
        i, n = code // 4, code & 3
        slot = (y - i) & 3
        old = (slot + step) & 3
        dv = nn(prob_ref[...], p_ref[i, ROWS : 2 * ROWS, :])
        dk = nn(ds_ref[...], p_ref[i, 0:ROWS, :]) * FACTOR
        acc_ref[i] += nn(k_ref[code].T, ds_ref[...])
        for kind, grad in ((0, dk), (1, dv)):
            dprev[n, old, kind] = (dprev[n, old, kind].astype(F32) + grad[:B]).astype(BF16)
            dcur[n, slot, kind] = (dcur[n, slot, kind].astype(F32) + grad[B:]).astype(BF16)

    @pl.when(count > 0)
    def _():
        before(0, p0, s0)

        def two(u, carry):
            before(2 * u + 1, p1, s1)
            after(2 * u, p0, s0)
            before(2 * u + 2, p0, s0)
            after(2 * u + 1, p1, s1)
            return carry

        lax.fori_loop(0, (count + 1) // 2, two, 0)


def merge(cur_ref, late_ref, *outs):
    for n in range(3):
        outs[n][...] = (cur_ref[n].astype(F32) + late_ref[n].astype(F32)).astype(BF16)


def gather_terms(*refs):
    terms, outs = refs[:-4], refs[-4:]
    for slot in range(4):
        total = terms[0][slot].astype(F32)
        for term in terms[1:]:
            total = total + term[slot].astype(F32)
        outs[slot][...] = total.astype(BF16)


def finish_q(d0, d1, d2, d3, out):
    y = lax.axis_index("y")
    for d, ref in enumerate((d0, d1, d2, d3)):
        head = lax.rem(y + d, 4)
        for g in range(GROUP):
            cols = pl.ds(pl.multiple_of((head * GROUP + g) * HD, HD), HD)
            out[:, cols] = ref[g * B : (g + 1) * B, :]


def finish_kv(d0, d1, d2, d3, k_out, v_out):
    y = lax.axis_index("y")
    for d, ref in enumerate((d0, d1, d2, d3)):
        cols = pl.ds(pl.multiple_of(lax.rem(y + d, 4) * HD, HD), HD)
        k_out[:, cols] = ref[0]
        v_out[:, cols] = ref[1]


def ring(x, axis, step, count):
    return lax.ppermute(x, axis, [(j, (j + step) % count) for j in range(count)])


def step(queries, keys, values, forward_out, logsumexp, upstream, lengths, sibling_mask):
    kv = shape((4, 2, B, HD), BF16)
    piece = shape((2, B, HD), BF16)
    row = shape((B, 512), BF16)
    core = ("x", "c")
    dists = (1, 2, 3)
    kv_sent = call(prep_kv, (piece,) * 4, 0, 2)(keys[0], values[0])
    kv_own = jnp.stack([kv_sent[0]] + [ring(kv_sent[d], "y", d, 4) for d in dists])
    qo_sent = call(prep_qo, (shape((QO, HD), BF16),) * 4, 1, 3)(
        sibling_mask.reshape(3), queries[0], forward_out[0], logsumexp.reshape(4, GROUP, B)
    )
    qo = [qo_sent[0]] + [ring(qo_sent[d], "y", d, 4) for d in dists]
    near = {0: kv_own, 1: ring(kv_own, "x", 1, 4), 3: ring(kv_own, "x", -1, 4)}
    near[2] = ring(near[3], "x", -1, 4)
    cur = [ring(kv_own, "z", d, 4) for d in dists]
    dealt = call(deal, shape((128, 16, HD), BF16), 0, 1, [pltpu.VMEM((128, 16, HD), F32)])(
        upstream.reshape(128, 2048)
    )
    arrived = lax.all_to_all(dealt, ("z", "y", "x", "c"), 0, 0, tiled=True)
    far = [ring(near[d], "c", 1, 2) for d in range(4)]
    prev = [ring(k, core, 1, 8) for k in cur]
    pay, stat, mark = call(
        prepare,
        (shape((4, 2 * ROWS, HD), BF16), shape((4, 2, ROWS), F32), shape((4, 8, HD), F32)),
        1,
        5,
        [pltpu.VMEM((128, 16, HD), F32)],
    )(lengths, arrived, *qo)
    mine, other, dq = {}, {}, None
    mine[0], other[0], dq = make_own(0, True, False)(pay, stat, near[0], far[0])
    mine[2], other[2], dq = make_own(2, False, False)(pay, stat, near[2], far[2], dq)
    trio = shape((3, 4, 2, B, HD), BF16)
    scratch = [pltpu.VMEM((16, 2 * B, HD), BF16)] * 2 + [pltpu.SMEM((16,), jnp.int32)]
    scratch += [pltpu.VMEM((2 * B, ROWS), BF16)] * 4
    sibling = call(sibling_kernel, (trio, trio, shape((4, HD, ROWS), F32)), 1, 10, scratch, {4: 2})
    dcur, dprev, dq = sibling(lengths, pay, stat, mark, dq, *cur, *prev)
    mine[3], other[3], dq = make_own(3, False, False)(pay, stat, near[3], far[3], dq)
    mine[1], other[1], *dq_sent = make_own(1, False, True)(pay, stat, near[1], far[1], dq)
    terms = [mine[0], ring(other[0], "c", 1, 2)]
    both = {d: mine[d].astype(F32) + ring(other[d], "c", 1, 2).astype(F32) for d in dists}
    passing = ring(both[2].astype(BF16), "x", 1, 4)
    joined = (both[3] + passing.astype(F32)).astype(BF16)
    terms.append(ring(joined, "x", 1, 4))
    terms.append(ring(both[1].astype(BF16), "x", -1, 4))
    late = ring(dprev, core, -1, 8)
    merged = call(merge, (kv,) * 3, 0, 2)(dcur, late)
    terms += [ring(merged[d - 1], "z", -d, 4) for d in dists]
    dq_got = [dq_sent[0]] + [ring(dq_sent[d], "y", -d, 4) for d in dists]
    q_grad = call(finish_q, (shape((B, 2048), BF16),), 0, 4)(*dq_got)[0]
    kv_out = call(gather_terms, (piece,) * 4, 0, 7)(*terms)
    kv_got = [kv_out[0]] + [ring(kv_out[d], "y", -d, 4) for d in dists]
    k_grad, v_grad = call(finish_kv, (row, row), 0, 4)(*kv_got)
    return q_grad[None], k_grad[None], v_grad[None]


def solution(mesh):
    grid = Mesh(mesh.devices.reshape(4, 4, 4, 2), ("z",) + SEQ)
    rows = P("z", SEQ, None)
    return jax.shard_map(
        step,
        mesh=grid,
        in_specs=(
            rows,
            rows,
            rows,
            rows,
            P("z", None, SEQ),
            P(None, ("z",) + SEQ, None),
            P(),
            P("z", None, SEQ),
        ),
        out_specs=(rows, rows, rows),
        check_vma=False,
    )
```

```python
import jax
import jax.numpy as jnp
from jax import lax
from jax.experimental import pallas as pl
from jax.experimental.pallas import tpu as pltpu
from jax.sharding import Mesh, PartitionSpec as P


B = 128
HD = 128
GROUP = 4
HEADS = 4
ROWS = GROUP * B
QO = 2 * ROWS + 16
FACTOR = HD**-0.5
LOG2E = 1.4426950408889634
SCALE = FACTOR * LOG2E
DEAD = 1e30
F32 = jnp.float32
BF16 = jnp.bfloat16
SEQ = ("y", "x", "c")
VMEM = pl.BlockSpec(memory_space=pltpu.VMEM)
SMEM = pl.BlockSpec(memory_space=pltpu.SMEM)


def nt(a, b):
    return lax.dot_general(a, b, (((1,), (1,)), ((), ())), preferred_element_type=F32)


def nn(a, b):
    return jnp.dot(a, b, preferred_element_type=F32)


def call(kernel, outs, n_smem, n_vmem, scratch=(), aliases=None):
    return pl.pallas_call(
        kernel,
        out_shape=outs,
        in_specs=[SMEM] * n_smem + [VMEM] * n_vmem,
        out_specs=jax.tree.map(lambda _: VMEM, outs),
        scratch_shapes=list(scratch),
        input_output_aliases=aliases or {},
        compiler_params=pltpu.CompilerParams(vmem_limit_bytes=48 << 20),
    )


def shape(dims, dtype):
    return jax.ShapeDtypeStruct(dims, dtype)


def prep_kv(k_ref, v_ref, *outs):
    y = lax.axis_index("y")
    for d in range(HEADS):
        cols = pl.ds(pl.multiple_of(lax.rem(y + d, 4) * HD, HD), HD)
        outs[d][0] = k_ref[:, cols]
        outs[d][1] = v_ref[:, cols]


def three(x):
    high = x.astype(BF16)
    rest = x - high.astype(F32)
    mid = rest.astype(BF16)
    low = (rest - mid.astype(F32)).astype(BF16)
    return [high.astype(F32), mid.astype(F32), low.astype(F32)]


def prep_qo(mask_ref, q_ref, o_ref, lse_ref, *outs):
    y = lax.axis_index("y")
    marks = [jnp.full((1, HD), mask_ref[n].astype(F32)) for n in range(3)] + [jnp.zeros((1, HD), F32)]
    for d in range(HEADS):
        head = lax.rem(y + d, 4)
        for g in range(GROUP):
            cols = pl.ds(pl.multiple_of((head * GROUP + g) * HD, HD), HD)
            outs[d][g * B : (g + 1) * B, :] = q_ref[:, cols]
            outs[d][ROWS + g * B : ROWS + (g + 1) * B, :] = o_ref[:, cols]
        outs[d][2 * ROWS : QO, :] = jnp.concatenate(three(lse_ref[head]) + marks, axis=0).astype(BF16)


def deal(up_ref, out_ref, wide_ref):
    for t in range(4):
        for c in range(4):
            for i in range(4):
                for g in range(GROUP):
                    cols = slice((c * GROUP + g) * HD, (c * GROUP + g + 1) * HD)
                    block = up_ref[(t * 4 + i) * 8 : (t * 4 + i + 1) * 8, cols]
                    wide_ref[(t * 4 + c) * 8 : (t * 4 + c + 1) * 8, i * GROUP + g, :] = block.astype(F32)
    out_ref[...] = wide_ref[...].astype(BF16)


def prepare(len_ref, g_ref, *refs):
    pieces, (p_ref, stat_ref, mark_ref, wide_ref) = refs[:4], refs[4:]
    y = lax.axis_index("y")
    length = len_ref[lax.axis_index("z")]
    shard = 2 * lax.axis_index("x") + lax.axis_index("c")
    lane = lax.broadcasted_iota(jnp.int32, (GROUP, B), 1)
    wide_ref[...] = g_ref[...].astype(F32)
    for n in range(16):
        p_ref[n // GROUP, ROWS + (n % GROUP) * B : ROWS + (n % GROUP + 1) * B, :] = wide_ref[:, n, :].astype(BF16)
    for d in range(4):
        i = lax.rem(y + 4 - d, 4)
        p_ref[i, 0:ROWS, :] = pieces[d][0:ROWS, :]
        raw = pieces[d][2 * ROWS : QO, :].astype(F32)
        lse = raw[0:4] + raw[4:8] + raw[8:12]
        lse = jnp.where((8 * i + shard) * B + lane < length, lse * LOG2E, DEAD)
        mark_ref[i] = raw[8:16]
        for g in range(GROUP):
            grad = p_ref[i, ROWS + g * B : ROWS + (g + 1) * B, :]
            out = pieces[d][ROWS + g * B : ROWS + (g + 1) * B, :]
            prod = grad.astype(F32) * out.astype(F32)
            stat_ref[i, 0:1, g * B : (g + 1) * B] = jnp.sum(prod.T, axis=0, keepdims=True)
            stat_ref[i, 1:2, g * B : (g + 1) * B] = lse[g : g + 1]


def weigh(keys, vals, p_ref, stat_ref, i, allow, prob_ref, ds_ref):
    q = p_ref[i, 0:ROWS, :]
    grad = p_ref[i, ROWS : 2 * ROWS, :]
    prob = jnp.exp2(nt(keys, q) * SCALE - stat_ref[i, 1:2, :])
    if allow is not None:
        prob = jnp.where(allow, prob, 0.0)
    diff = nt(vals, grad) - stat_ref[i, 0:1, :]
    prob_ref[...] = prob.astype(BF16)
    ds_ref[...] = (prob * diff).astype(BF16)


MS = sum(m << (2 * t) for t, m in enumerate((0, 0, 0, 1, 1, 2, 0, 1, 2, 3)))
QS = sum(i << (2 * t) for t, i in enumerate((1, 2, 3, 2, 3, 3, 0, 1, 2, 3)))


def make_own(dist, first, last):
    def kernel(p_ref, stat_ref, km_ref, ko_ref, *refs):
        if not first:
            dq_in, refs = refs[0], refs[1:]
        dm_ref, do_ref, refs = refs[0], refs[1], refs[2:]
        if last:
            dq_outs, refs = refs[:4], refs[4:]
            kt_ref, dk_ref, dv_ref, p0, s0, p1, s1, acc_ref = refs
        else:
            acc_ref, kt_ref, dk_ref, dv_ref, p0, s0, p1, s1 = refs
        chip = lax.axis_index("x")
        core = lax.axis_index("c")
        y = lax.axis_index("y")
        if first:
            acc_ref[...] = jnp.zeros_like(acc_ref)
        elif last:
            acc_ref[...] = dq_in[...]
        dk_ref[...] = jnp.zeros_like(dk_ref)
        dv_ref[...] = jnp.zeros_like(dv_ref)
        for m in range(4):
            kt_ref[m] = jnp.concatenate([km_ref[m, 0], ko_ref[m, 0]], axis=0).T
        if dist == 0:
            count = 10
        else:
            count = jnp.where(lax.rem(chip + 4 - dist, 4) < chip, 10, 6)

        def which(t):
            t = jnp.minimum(t, count - 1)
            m = lax.shift_right_logical(jnp.int32(MS), 2 * t) & 3
            i = lax.shift_right_logical(jnp.int32(QS), 2 * t) & 3
            return m, i, (y - m) & 3

        def before(t, prob_ref, ds_ref):
            m, i, slot = which(t)
            keys = jnp.concatenate([km_ref[slot, 0], ko_ref[slot, 0]], axis=0)
            vals = jnp.concatenate([km_ref[slot, 1], ko_ref[slot, 1]], axis=0)
            allow = None
            if dist == 0:
                row = lax.broadcasted_iota(jnp.int32, (2 * B, ROWS), 0)
                col = lax.broadcasted_iota(jnp.int32, (1, ROWS), 1)
                row = jnp.where(core == 0, row, row ^ B)
                allow = row <= core * B + col % B + jnp.where(i > m, 4 * B, 0)
            weigh(keys, vals, p_ref, stat_ref, i, allow, prob_ref, ds_ref)

        def after(t, prob_ref, ds_ref):
            _, i, slot = which(t)
            dv_ref[slot] += nn(prob_ref[...], p_ref[i, ROWS : 2 * ROWS, :])
            dk_ref[slot] += nn(ds_ref[...], p_ref[i, 0:ROWS, :])
            acc_ref[i] += nn(kt_ref[slot], ds_ref[...])

        before(0, p0, s0)

        def two(u, carry):
            before(2 * u + 1, p1, s1)
            after(2 * u, p0, s0)
            before(2 * u + 2, p0, s0)
            after(2 * u + 1, p1, s1)
            return carry

        lax.fori_loop(0, count // 2, two, 0)
        for m in range(4):
            dk = (dk_ref[m] * FACTOR).astype(BF16)
            dv = dv_ref[m].astype(BF16)
            dm_ref[m, 0] = dk[:B]
            dm_ref[m, 1] = dv[:B]
            do_ref[m, 0] = dk[B:]
            do_ref[m, 1] = dv[B:]
        if last:
            for d in range(4):
                dq_outs[d][...] = (acc_ref[(y - d) & 3].T * FACTOR).astype(BF16)

    kv = shape((4, 2, B, HD), BF16)
    dq = [shape((ROWS, HD), BF16)] * 4 if last else [shape((4, HD, ROWS), F32)]
    scratch = [
        pltpu.VMEM((4, HD, 2 * B), BF16),
        pltpu.VMEM((4, 2 * B, HD), F32),
        pltpu.VMEM((4, 2 * B, HD), F32),
    ] + [pltpu.VMEM((2 * B, ROWS), BF16)] * 4
    if last:
        scratch.append(pltpu.VMEM((4, HD, ROWS), F32))
    aliases = None if first or last else {4: 2}
    return call(kernel, (kv, kv, *dq), 0, 4 if first else 5, scratch, aliases)


def sibling_kernel(len_ref, p_ref, stat_ref, mark_ref, dq_in, *refs):
    cur, prev, refs = refs[0:3], refs[3:6], refs[6:]
    dcur, dprev, acc_ref, k_ref, v_ref, list_ref, p0, s0, p1, s1 = refs
    thinker = lax.axis_index("z")
    y = lax.axis_index("y")
    shard = 2 * lax.axis_index("x") + lax.axis_index("c")
    length = len_ref[thinker]
    del dq_in
    dcur[...] = jnp.zeros_like(dcur)
    dprev[...] = jnp.zeros_like(dprev)
    step = (shard == 0).astype(jnp.int32)
    count = jnp.int32(0)
    for i in range(4):
        slot = (y - i) & 3
        old = (slot + step) & 3
        block = 8 * i + shard
        for n in range(3):
            code = i * 4 + n
            k_ref[code, :B] = prev[n][old, 0]
            k_ref[code, B:] = cur[n][slot, 0]
            v_ref[code, :B] = prev[n][old, 1]
            v_ref[code, B:] = cur[n][slot, 1]
            top = len_ref[(thinker - 1 - n) & 3] - (block - 1) * B
            wanted = jnp.max(mark_ref[i, 6 - n : 7 - n, :]) > 0.5
            list_ref[count] = code
            count = count + (wanted & (block * B < length) & (top > 0)).astype(jnp.int32)
    list_ref[count] = 0
    list_ref[count + 1] = 0
    list_ref[count + 2] = 0

    def before(t, prob_ref, ds_ref):
        code = list_ref[t]
        i, n = code // 4, code & 3
        block = 8 * i + shard
        top = len_ref[(thinker - 1 - n) & 3] - (block - 1) * B
        low = jnp.where(block == 0, B, 0)
        top = jnp.where(t < count, top, 0)
        row = lax.broadcasted_iota(jnp.int32, (2 * B, ROWS), 0)
        col = lax.broadcasted_iota(jnp.int32, (1, ROWS), 1) % B
        allow = (row > jnp.maximum(col, low - 1)) & (row <= jnp.minimum(col + B, top - 1))
        weigh(k_ref[code], v_ref[code], p_ref, stat_ref, i, allow, prob_ref, ds_ref)

    def after(t, prob_ref, ds_ref):
        code = list_ref[t]
        i, n = code // 4, code & 3
        slot = (y - i) & 3
        old = (slot + step) & 3
        dv = nn(prob_ref[...], p_ref[i, ROWS : 2 * ROWS, :])
        dk = nn(ds_ref[...], p_ref[i, 0:ROWS, :]) * FACTOR
        acc_ref[i] += nn(k_ref[code].T, ds_ref[...])
        for kind, grad in ((0, dk), (1, dv)):
            dprev[n, old, kind] = (dprev[n, old, kind].astype(F32) + grad[:B]).astype(BF16)
            dcur[n, slot, kind] = (dcur[n, slot, kind].astype(F32) + grad[B:]).astype(BF16)

    @pl.when(count > 0)
    def _():
        before(0, p0, s0)

        def two(u, carry):
            before(2 * u + 1, p1, s1)
            after(2 * u, p0, s0)
            before(2 * u + 2, p0, s0)
            after(2 * u + 1, p1, s1)
            return carry

        lax.fori_loop(0, (count + 1) // 2, two, 0)


def merge(cur_ref, late_ref, *outs):
    for n in range(3):
        outs[n][...] = (cur_ref[n].astype(F32) + late_ref[n].astype(F32)).astype(BF16)


def gather_terms(*refs):
    terms, outs = refs[:-4], refs[-4:]
    for slot in range(4):
        total = terms[0][slot].astype(F32)
        for term in terms[1:]:
            total = total + term[slot].astype(F32)
        outs[slot][...] = total.astype(BF16)


def finish_q(d0, d1, d2, d3, out):
    y = lax.axis_index("y")
    for d, ref in enumerate((d0, d1, d2, d3)):
        head = lax.rem(y + d, 4)
        for g in range(GROUP):
            cols = pl.ds(pl.multiple_of((head * GROUP + g) * HD, HD), HD)
            out[:, cols] = ref[g * B : (g + 1) * B, :]


def finish_kv(d0, d1, d2, d3, k_out, v_out):
    y = lax.axis_index("y")
    for d, ref in enumerate((d0, d1, d2, d3)):
        cols = pl.ds(pl.multiple_of(lax.rem(y + d, 4) * HD, HD), HD)
        k_out[:, cols] = ref[0]
        v_out[:, cols] = ref[1]


def ring(x, axis, step, count):
    return lax.ppermute(x, axis, [(j, (j + step) % count) for j in range(count)])


def step(queries, keys, values, forward_out, logsumexp, upstream, lengths, sibling_mask):
    kv = shape((4, 2, B, HD), BF16)
    piece = shape((2, B, HD), BF16)
    row = shape((B, 512), BF16)
    core = ("x", "c")
    dists = (1, 2, 3)
    kv_sent = call(prep_kv, (piece,) * 4, 0, 2)(keys[0], values[0])
    kv_own = jnp.stack([kv_sent[0]] + [ring(kv_sent[d], "y", d, 4) for d in dists])
    qo_sent = call(prep_qo, (shape((QO, HD), BF16),) * 4, 1, 3)(
        sibling_mask.reshape(3), queries[0], forward_out[0], logsumexp.reshape(4, GROUP, B)
    )
    qo = [qo_sent[0]] + [ring(qo_sent[d], "y", d, 4) for d in dists]
    near = {0: kv_own, 1: ring(kv_own, "x", 1, 4), 3: ring(kv_own, "x", -1, 4)}
    near[2] = ring(near[3], "x", -1, 4)
    cur = [ring(kv_own, "z", d, 4) for d in dists]
    dealt = call(deal, shape((128, 16, HD), BF16), 0, 1, [pltpu.VMEM((128, 16, HD), F32)])(
        upstream.reshape(128, 2048)
    )
    arrived = lax.all_to_all(dealt, ("z", "y", "x", "c"), 0, 0, tiled=True)
    far = [ring(near[d], "c", 1, 2) for d in range(4)]
    prev = [ring(k, core, 1, 8) for k in cur]
    pay, stat, mark = call(
        prepare,
        (shape((4, 2 * ROWS, HD), BF16), shape((4, 2, ROWS), F32), shape((4, 8, HD), F32)),
        1,
        5,
        [pltpu.VMEM((128, 16, HD), F32)],
    )(lengths, arrived, *qo)
    mine, other, dq = {}, {}, None
    mine[3], other[3], dq = make_own(3, True, False)(pay, stat, near[3], far[3])
    mine[2], other[2], dq = make_own(2, False, False)(pay, stat, near[2], far[2], dq)
    trio = shape((3, 4, 2, B, HD), BF16)
    scratch = [pltpu.VMEM((16, 2 * B, HD), BF16)] * 2 + [pltpu.SMEM((16,), jnp.int32)]
    scratch += [pltpu.VMEM((2 * B, ROWS), BF16)] * 4
    sibling = call(sibling_kernel, (trio, trio, shape((4, HD, ROWS), F32)), 1, 10, scratch, {4: 2})
    dcur, dprev, dq = sibling(lengths, pay, stat, mark, dq, *cur, *prev)
    mine[1], other[1], dq = make_own(1, False, False)(pay, stat, near[1], far[1], dq)
    mine[0], other[0], *dq_sent = make_own(0, False, True)(pay, stat, near[0], far[0], dq)
    terms = [mine[0], ring(other[0], "c", 1, 2)]
    both = {d: mine[d].astype(F32) + ring(other[d], "c", 1, 2).astype(F32) for d in dists}
    passing = ring(both[2].astype(BF16), "x", 1, 4)
    joined = (both[3] + passing.astype(F32)).astype(BF16)
    terms.append(ring(joined, "x", 1, 4))
    terms.append(ring(both[1].astype(BF16), "x", -1, 4))
    late = ring(dprev, core, -1, 8)
    merged = call(merge, (kv,) * 3, 0, 2)(dcur, late)
    terms += [ring(merged[d - 1], "z", -d, 4) for d in dists]
    dq_got = [dq_sent[0]] + [ring(dq_sent[d], "y", -d, 4) for d in dists]
    q_grad = call(finish_q, (shape((B, 2048), BF16),), 0, 4)(*dq_got)[0]
    kv_out = call(gather_terms, (piece,) * 4, 0, 7)(*terms)
    kv_got = [kv_out[0]] + [ring(kv_out[d], "y", -d, 4) for d in dists]
    k_grad, v_grad = call(finish_kv, (row, row), 0, 4)(*kv_got)
    return q_grad[None], k_grad[None], v_grad[None]


def solution(mesh):
    grid = Mesh(mesh.devices.reshape(4, 4, 4, 2), ("z",) + SEQ)
    rows = P("z", SEQ, None)
    return jax.shard_map(
        step,
        mesh=grid,
        in_specs=(
            rows,
            rows,
            rows,
            rows,
            P("z", None, SEQ),
            P(None, ("z",) + SEQ, None),
            P(),
            P("z", None, SEQ),
        ),
        out_specs=(rows, rows, rows),
        check_vma=False,
    )
```

```python
import jax
import jax.numpy as jnp
from jax import lax
from jax.experimental import pallas as pl
from jax.experimental.pallas import tpu as pltpu
from jax.sharding import Mesh, PartitionSpec as P


B = 128
HD = 128
GROUP = 4
HEADS = 4
ROWS = GROUP * B
QO = 2 * ROWS + 16
FACTOR = HD**-0.5
LOG2E = 1.4426950408889634
SCALE = FACTOR * LOG2E
DEAD = 1e30
F32 = jnp.float32
BF16 = jnp.bfloat16
SEQ = ("y", "x", "c")
VMEM = pl.BlockSpec(memory_space=pltpu.VMEM)
SMEM = pl.BlockSpec(memory_space=pltpu.SMEM)


def nt(a, b):
    return lax.dot_general(a, b, (((1,), (1,)), ((), ())), preferred_element_type=F32)


def nn(a, b):
    return jnp.dot(a, b, preferred_element_type=F32)


def call(kernel, outs, n_smem, n_vmem, scratch=(), aliases=None):
    return pl.pallas_call(
        kernel,
        out_shape=outs,
        in_specs=[SMEM] * n_smem + [VMEM] * n_vmem,
        out_specs=jax.tree.map(lambda _: VMEM, outs),
        scratch_shapes=list(scratch),
        input_output_aliases=aliases or {},
        compiler_params=pltpu.CompilerParams(vmem_limit_bytes=48 << 20),
    )


def shape(dims, dtype):
    return jax.ShapeDtypeStruct(dims, dtype)


def prep_kv(k_ref, v_ref, *outs):
    y = lax.axis_index("y")
    for d in range(HEADS):
        cols = pl.ds(pl.multiple_of(lax.rem(y + d, 4) * HD, HD), HD)
        outs[d][0] = k_ref[:, cols]
        outs[d][1] = v_ref[:, cols]


def three(x):
    high = x.astype(BF16)
    rest = x - high.astype(F32)
    mid = rest.astype(BF16)
    low = (rest - mid.astype(F32)).astype(BF16)
    return [high.astype(F32), mid.astype(F32), low.astype(F32)]


def prep_qo(mask_ref, q_ref, o_ref, lse_ref, *outs):
    y = lax.axis_index("y")
    marks = [jnp.full((1, HD), mask_ref[n].astype(F32)) for n in range(3)] + [jnp.zeros((1, HD), F32)]
    for d in range(HEADS):
        head = lax.rem(y + d, 4)
        for g in range(GROUP):
            cols = pl.ds(pl.multiple_of((head * GROUP + g) * HD, HD), HD)
            outs[d][g * B : (g + 1) * B, :] = q_ref[:, cols]
            outs[d][ROWS + g * B : ROWS + (g + 1) * B, :] = o_ref[:, cols]
        outs[d][2 * ROWS : QO, :] = jnp.concatenate(three(lse_ref[head]) + marks, axis=0).astype(BF16)


def deal(up_ref, out_ref, wide_ref):
    for t in range(4):
        for c in range(4):
            for i in range(4):
                for g in range(GROUP):
                    cols = slice((c * GROUP + g) * HD, (c * GROUP + g + 1) * HD)
                    block = up_ref[(t * 4 + i) * 8 : (t * 4 + i + 1) * 8, cols]
                    wide_ref[(t * 4 + c) * 8 : (t * 4 + c + 1) * 8, i * GROUP + g, :] = block.astype(F32)
    out_ref[...] = wide_ref[...].astype(BF16)


def unpack(g_ref, grad_ref, wide_ref):
    wide_ref[...] = g_ref[...].astype(F32)
    for n in range(16):
        g = n % GROUP
        grad_ref[n // GROUP, g * B : (g + 1) * B, :] = wide_ref[:, n, :].astype(BF16)


def prepare(len_ref, grad_ref, *refs):
    pieces, (q_ref, stat_ref, mark_ref) = refs[:4], refs[4:]
    y = lax.axis_index("y")
    length = len_ref[lax.axis_index("z")]
    shard = 2 * lax.axis_index("x") + lax.axis_index("c")
    lane = lax.broadcasted_iota(jnp.int32, (GROUP, B), 1)
    for d in range(4):
        i = lax.rem(y + 4 - d, 4)
        q_ref[i] = pieces[d][0:ROWS, :]
        raw = pieces[d][2 * ROWS : QO, :].astype(F32)
        lse = raw[0:4] + raw[4:8] + raw[8:12]
        lse = jnp.where((8 * i + shard) * B + lane < length, lse * LOG2E, DEAD)
        mark_ref[i] = raw[8:16]
        for g in range(GROUP):
            rows = slice(g * B, (g + 1) * B)
            out = pieces[d][ROWS + g * B : ROWS + (g + 1) * B, :]
            prod = grad_ref[i, rows, :].astype(F32) * out.astype(F32)
            stat_ref[i, 0:1, rows] = jnp.sum(prod.T, axis=0, keepdims=True)
            stat_ref[i, 1:2, rows] = lse[g : g + 1]


def weigh(keys, vals, q_ref, grad_ref, stat_ref, i, allow, prob_ref, ds_ref):
    q = q_ref[i]
    grad = grad_ref[i]
    prob = jnp.exp2(nt(keys, q) * SCALE - stat_ref[i, 1:2, :])
    if allow is not None:
        prob = jnp.where(allow, prob, 0.0)
    diff = nt(vals, grad) - stat_ref[i, 0:1, :]
    prob_ref[...] = prob.astype(BF16)
    ds_ref[...] = (prob * diff).astype(BF16)


MS = sum(m << (2 * t) for t, m in enumerate((0, 0, 0, 1, 1, 2, 0, 1, 2, 3)))
QS = sum(i << (2 * t) for t, i in enumerate((1, 2, 3, 2, 3, 3, 0, 1, 2, 3)))


def make_own(dist, first, last):
    def kernel(q_ref, grad_ref, stat_ref, km_ref, ko_ref, *refs):
        if not first:
            dq_in, refs = refs[0], refs[1:]
        dm_ref, do_ref, refs = refs[0], refs[1], refs[2:]
        if last:
            dq_outs, refs = refs[:4], refs[4:]
            kt_ref, dk_ref, dv_ref, p0, s0, p1, s1, acc_ref = refs
        else:
            acc_ref, kt_ref, dk_ref, dv_ref, p0, s0, p1, s1 = refs
        chip = lax.axis_index("x")
        core = lax.axis_index("c")
        y = lax.axis_index("y")
        if first:
            acc_ref[...] = jnp.zeros_like(acc_ref)
        elif last:
            acc_ref[...] = dq_in[...]
        dk_ref[...] = jnp.zeros_like(dk_ref)
        dv_ref[...] = jnp.zeros_like(dv_ref)
        for m in range(4):
            kt_ref[m] = jnp.concatenate([km_ref[m, 0], ko_ref[m, 0]], axis=0).T
        if dist == 0:
            count = 10
        else:
            count = jnp.where(lax.rem(chip + 4 - dist, 4) < chip, 10, 6)

        def which(t):
            t = jnp.minimum(t, count - 1)
            m = lax.shift_right_logical(jnp.int32(MS), 2 * t) & 3
            i = lax.shift_right_logical(jnp.int32(QS), 2 * t) & 3
            return m, i, (y - m) & 3

        def before(t, prob_ref, ds_ref):
            m, i, slot = which(t)
            keys = jnp.concatenate([km_ref[slot, 0], ko_ref[slot, 0]], axis=0)
            vals = jnp.concatenate([km_ref[slot, 1], ko_ref[slot, 1]], axis=0)
            allow = None
            if dist == 0:
                row = lax.broadcasted_iota(jnp.int32, (2 * B, ROWS), 0)
                col = lax.broadcasted_iota(jnp.int32, (1, ROWS), 1)
                row = jnp.where(core == 0, row, row ^ B)
                allow = row <= core * B + col % B + jnp.where(i > m, 4 * B, 0)
            weigh(keys, vals, q_ref, grad_ref, stat_ref, i, allow, prob_ref, ds_ref)

        def after(t, prob_ref, ds_ref):
            _, i, slot = which(t)
            dv_ref[slot] += nn(prob_ref[...], grad_ref[i])
            dk_ref[slot] += nn(ds_ref[...], q_ref[i])
            acc_ref[i] += nn(kt_ref[slot], ds_ref[...])

        before(0, p0, s0)

        def two(u, carry):
            before(2 * u + 1, p1, s1)
            after(2 * u, p0, s0)
            before(2 * u + 2, p0, s0)
            after(2 * u + 1, p1, s1)
            return carry

        lax.fori_loop(0, count // 2, two, 0)
        for m in range(4):
            dk = (dk_ref[m] * FACTOR).astype(BF16)
            dv = dv_ref[m].astype(BF16)
            dm_ref[m, 0] = dk[:B]
            dm_ref[m, 1] = dv[:B]
            do_ref[m, 0] = dk[B:]
            do_ref[m, 1] = dv[B:]
        if last:
            for d in range(4):
                dq_outs[d][...] = (acc_ref[(y - d) & 3].T * FACTOR).astype(BF16)

    kv = shape((4, 2, B, HD), BF16)
    dq = [shape((ROWS, HD), BF16)] * 4 if last else [shape((4, HD, ROWS), F32)]
    scratch = [
        pltpu.VMEM((4, HD, 2 * B), BF16),
        pltpu.VMEM((4, 2 * B, HD), F32),
        pltpu.VMEM((4, 2 * B, HD), F32),
    ] + [pltpu.VMEM((2 * B, ROWS), BF16)] * 4
    if last:
        scratch.append(pltpu.VMEM((4, HD, ROWS), F32))
    aliases = None if first or last else {5: 2}
    return call(kernel, (kv, kv, *dq), 0, 5 if first else 6, scratch, aliases)


def sibling_kernel(len_ref, q_ref, grad_ref, stat_ref, mark_ref, dq_in, *refs):
    cur, prev, refs = refs[0:3], refs[3:6], refs[6:]
    dcur, dprev, acc_ref, k_ref, v_ref, list_ref, p0, s0, p1, s1 = refs
    thinker = lax.axis_index("z")
    y = lax.axis_index("y")
    shard = 2 * lax.axis_index("x") + lax.axis_index("c")
    length = len_ref[thinker]
    del dq_in
    dcur[...] = jnp.zeros_like(dcur)
    dprev[...] = jnp.zeros_like(dprev)
    step = (shard == 0).astype(jnp.int32)
    count = jnp.int32(0)
    for i in range(4):
        slot = (y - i) & 3
        old = (slot + step) & 3
        block = 8 * i + shard
        for n in range(3):
            code = i * 4 + n
            k_ref[code, :B] = prev[n][old, 0]
            k_ref[code, B:] = cur[n][slot, 0]
            v_ref[code, :B] = prev[n][old, 1]
            v_ref[code, B:] = cur[n][slot, 1]
            top = len_ref[(thinker - 1 - n) & 3] - (block - 1) * B
            wanted = jnp.max(mark_ref[i, 6 - n : 7 - n, :]) > 0.5
            list_ref[count] = code
            count = count + (wanted & (block * B < length) & (top > 0)).astype(jnp.int32)
    list_ref[count] = 0
    list_ref[count + 1] = 0
    list_ref[count + 2] = 0

    def before(t, prob_ref, ds_ref):
        code = list_ref[t]
        i, n = code // 4, code & 3
        block = 8 * i + shard
        top = len_ref[(thinker - 1 - n) & 3] - (block - 1) * B
        low = jnp.where(block == 0, B, 0)
        top = jnp.where(t < count, top, 0)
        row = lax.broadcasted_iota(jnp.int32, (2 * B, ROWS), 0)
        col = lax.broadcasted_iota(jnp.int32, (1, ROWS), 1) % B
        allow = (row > jnp.maximum(col, low - 1)) & (row <= jnp.minimum(col + B, top - 1))
        weigh(k_ref[code], v_ref[code], q_ref, grad_ref, stat_ref, i, allow, prob_ref, ds_ref)

    def after(t, prob_ref, ds_ref):
        code = list_ref[t]
        i, n = code // 4, code & 3
        slot = (y - i) & 3
        old = (slot + step) & 3
        dv = nn(prob_ref[...], grad_ref[i])
        dk = nn(ds_ref[...], q_ref[i]) * FACTOR
        acc_ref[i] += nn(k_ref[code].T, ds_ref[...])
        for kind, grad in ((0, dk), (1, dv)):
            dprev[n, old, kind] = (dprev[n, old, kind].astype(F32) + grad[:B]).astype(BF16)
            dcur[n, slot, kind] = (dcur[n, slot, kind].astype(F32) + grad[B:]).astype(BF16)

    @pl.when(count > 0)
    def _():
        before(0, p0, s0)

        def two(u, carry):
            before(2 * u + 1, p1, s1)
            after(2 * u, p0, s0)
            before(2 * u + 2, p0, s0)
            after(2 * u + 1, p1, s1)
            return carry

        lax.fori_loop(0, (count + 1) // 2, two, 0)


def merge(cur_ref, late_ref, *outs):
    for n in range(3):
        outs[n][...] = (cur_ref[n].astype(F32) + late_ref[n].astype(F32)).astype(BF16)


def gather_terms(*refs):
    terms, outs = refs[:-4], refs[-4:]
    for slot in range(4):
        total = terms[0][slot].astype(F32)
        for term in terms[1:]:
            total = total + term[slot].astype(F32)
        outs[slot][...] = total.astype(BF16)


def finish_q(d0, d1, d2, d3, out):
    y = lax.axis_index("y")
    for d, ref in enumerate((d0, d1, d2, d3)):
        head = lax.rem(y + d, 4)
        for g in range(GROUP):
            cols = pl.ds(pl.multiple_of((head * GROUP + g) * HD, HD), HD)
            out[:, cols] = ref[g * B : (g + 1) * B, :]


def finish_kv(d0, d1, d2, d3, k_out, v_out):
    y = lax.axis_index("y")
    for d, ref in enumerate((d0, d1, d2, d3)):
        cols = pl.ds(pl.multiple_of(lax.rem(y + d, 4) * HD, HD), HD)
        k_out[:, cols] = ref[0]
        v_out[:, cols] = ref[1]


def ring(x, axis, step, count):
    return lax.ppermute(x, axis, [(j, (j + step) % count) for j in range(count)])


def step(queries, keys, values, forward_out, logsumexp, upstream, lengths, sibling_mask):
    kv = shape((4, 2, B, HD), BF16)
    piece = shape((2, B, HD), BF16)
    row = shape((B, 512), BF16)
    core = ("x", "c")
    dists = (1, 2, 3)
    kv_sent = call(prep_kv, (piece,) * 4, 0, 2)(keys[0], values[0])
    kv_own = jnp.stack([kv_sent[0]] + [ring(kv_sent[d], "y", d, 4) for d in dists])
    qo_sent = call(prep_qo, (shape((QO, HD), BF16),) * 4, 1, 3)(
        sibling_mask.reshape(3), queries[0], forward_out[0], logsumexp.reshape(4, GROUP, B)
    )
    qo = [qo_sent[0]] + [ring(qo_sent[d], "y", d, 4) for d in dists]
    near = {0: kv_own, 1: ring(kv_own, "x", 1, 4), 3: ring(kv_own, "x", -1, 4)}
    near[2] = ring(near[3], "x", -1, 4)
    cur = [ring(kv_own, "z", d, 4) for d in dists]
    dealt = call(deal, shape((128, 16, HD), BF16), 0, 1, [pltpu.VMEM((128, 16, HD), F32)])(
        upstream.reshape(128, 2048)
    )
    arrived = lax.all_to_all(dealt, ("z", "y", "x", "c"), 0, 0, tiled=True)
    far = [ring(near[d], "c", 1, 2) for d in range(4)]
    prev = [ring(k, core, 1, 8) for k in cur]
    rows4 = shape((4, ROWS, HD), BF16)
    grads = call(unpack, rows4, 0, 1, [pltpu.VMEM((128, 16, HD), F32)])(arrived)
    query, stat, mark = call(
        prepare, (rows4, shape((4, 2, ROWS), F32), shape((4, 8, HD), F32)), 1, 5
    )(lengths, grads, *qo)
    rows_in = (query, grads, stat)
    mine, other, dq = {}, {}, None
    mine[3], other[3], dq = make_own(3, True, False)(*rows_in, near[3], far[3])
    mine[2], other[2], dq = make_own(2, False, False)(*rows_in, near[2], far[2], dq)
    trio = shape((3, 4, 2, B, HD), BF16)
    scratch = [pltpu.VMEM((16, 2 * B, HD), BF16)] * 2 + [pltpu.SMEM((16,), jnp.int32)]
    scratch += [pltpu.VMEM((2 * B, ROWS), BF16)] * 4
    sibling = call(sibling_kernel, (trio, trio, shape((4, HD, ROWS), F32)), 1, 11, scratch, {5: 2})
    dcur, dprev, dq = sibling(lengths, *rows_in, mark, dq, *cur, *prev)
    mine[1], other[1], dq = make_own(1, False, False)(*rows_in, near[1], far[1], dq)
    mine[0], other[0], *dq_sent = make_own(0, False, True)(*rows_in, near[0], far[0], dq)
    terms = [mine[0], ring(other[0], "c", 1, 2)]
    moved = {d: ring(other[d], "c", 1, 2).astype(F32) for d in dists}
    passing = ring((mine[2].astype(F32) + moved[2]).astype(BF16), "x", 1, 4)
    joined = (mine[3].astype(F32) + moved[3] + passing.astype(F32)).astype(BF16)
    nearest = (mine[1].astype(F32) + moved[1]).astype(BF16)
    terms.append(ring(joined, "x", 1, 4))
    terms.append(ring(nearest, "x", -1, 4))
    late = ring(dprev, core, -1, 8)
    merged = call(merge, (kv,) * 3, 0, 2)(dcur, late)
    terms += [ring(merged[d - 1], "z", -d, 4) for d in dists]
    dq_got = [dq_sent[0]] + [ring(dq_sent[d], "y", -d, 4) for d in dists]
    q_grad = call(finish_q, (shape((B, 2048), BF16),), 0, 4)(*dq_got)[0]
    kv_out = call(gather_terms, (piece,) * 4, 0, 7)(*terms)
    kv_got = [kv_out[0]] + [ring(kv_out[d], "y", -d, 4) for d in dists]
    k_grad, v_grad = call(finish_kv, (row, row), 0, 4)(*kv_got)
    return q_grad[None], k_grad[None], v_grad[None]


def solution(mesh):
    grid = Mesh(mesh.devices.reshape(4, 4, 4, 2), ("z",) + SEQ)
    rows = P("z", SEQ, None)
    return jax.shard_map(
        step,
        mesh=grid,
        in_specs=(
            rows,
            rows,
            rows,
            rows,
            P("z", None, SEQ),
            P(None, ("z",) + SEQ, None),
            P(),
            P("z", None, SEQ),
        ),
        out_specs=(rows, rows, rows),
        check_vma=False,
    )
```

```python
import jax
import jax.numpy as jnp
from jax import lax
from jax.experimental import pallas as pl
from jax.experimental.pallas import tpu as pltpu
from jax.sharding import Mesh, PartitionSpec as P


B = 128
HD = 128
GROUP = 4
HEADS = 4
ROWS = GROUP * B
QO = 2 * ROWS + 16
FACTOR = HD**-0.5
LOG2E = 1.4426950408889634
SCALE = FACTOR * LOG2E
DEAD = 1e30
F32 = jnp.float32
BF16 = jnp.bfloat16
SEQ = ("y", "x", "c")
VMEM = pl.BlockSpec(memory_space=pltpu.VMEM)
SMEM = pl.BlockSpec(memory_space=pltpu.SMEM)


def nt(a, b):
    return lax.dot_general(a, b, (((1,), (1,)), ((), ())), preferred_element_type=F32)


def nn(a, b):
    return jnp.dot(a, b, preferred_element_type=F32)


def call(kernel, outs, n_smem, n_vmem, scratch=(), aliases=None):
    return pl.pallas_call(
        kernel,
        out_shape=outs,
        in_specs=[SMEM] * n_smem + [VMEM] * n_vmem,
        out_specs=jax.tree.map(lambda _: VMEM, outs),
        scratch_shapes=list(scratch),
        input_output_aliases=aliases or {},
        compiler_params=pltpu.CompilerParams(vmem_limit_bytes=48 << 20),
    )


def shape(dims, dtype):
    return jax.ShapeDtypeStruct(dims, dtype)


def prep_kv(k_ref, v_ref, *outs):
    y = lax.axis_index("y")
    for d in range(HEADS):
        cols = pl.ds(pl.multiple_of(lax.rem(y + d, 4) * HD, HD), HD)
        outs[d][0] = k_ref[:, cols]
        outs[d][1] = v_ref[:, cols]


def three(x):
    high = x.astype(BF16)
    rest = x - high.astype(F32)
    mid = rest.astype(BF16)
    low = (rest - mid.astype(F32)).astype(BF16)
    return [high.astype(F32), mid.astype(F32), low.astype(F32)]


def prep_qo(mask_ref, q_ref, o_ref, lse_ref, *outs):
    y = lax.axis_index("y")
    marks = [jnp.full((1, HD), mask_ref[n].astype(F32)) for n in range(3)] + [jnp.zeros((1, HD), F32)]
    for d in range(HEADS):
        head = lax.rem(y + d, 4)
        for g in range(GROUP):
            cols = pl.ds(pl.multiple_of((head * GROUP + g) * HD, HD), HD)
            outs[d][g * B : (g + 1) * B, :] = q_ref[:, cols]
            outs[d][ROWS + g * B : ROWS + (g + 1) * B, :] = o_ref[:, cols]
        outs[d][2 * ROWS : QO, :] = jnp.concatenate(three(lse_ref[head]) + marks, axis=0).astype(BF16)


def deal(up_ref, out_ref, wide_ref):
    for c in range(4):
        for i in range(4):
            for g in range(GROUP):
                cols = slice((c * GROUP + g) * HD, (c * GROUP + g + 1) * HD)
                block = up_ref[i * 8 : (i + 1) * 8, cols]
                wide_ref[c * 8 : (c + 1) * 8, i * GROUP + g, :] = block.astype(F32)
    out_ref[...] = wide_ref[...].astype(BF16)


def unpack(g_ref, grad_ref, wide_ref):
    wide_ref[...] = g_ref[...].astype(F32)
    for n in range(16):
        g = n % GROUP
        grad_ref[n // GROUP, g * B : (g + 1) * B, :] = wide_ref[:, n, :].astype(BF16)


def prepare(len_ref, grad_ref, *refs):
    pieces, (q_ref, stat_ref, mark_ref) = refs[:4], refs[4:]
    y = lax.axis_index("y")
    length = len_ref[lax.axis_index("z")]
    shard = 2 * lax.axis_index("x") + lax.axis_index("c")
    lane = lax.broadcasted_iota(jnp.int32, (GROUP, B), 1)
    for d in range(4):
        i = lax.rem(y + 4 - d, 4)
        q_ref[i] = pieces[d][0:ROWS, :]
        raw = pieces[d][2 * ROWS : QO, :].astype(F32)
        lse = raw[0:4] + raw[4:8] + raw[8:12]
        lse = jnp.where((8 * i + shard) * B + lane < length, lse * LOG2E, DEAD)
        mark_ref[i] = raw[8:16]
        for g in range(GROUP):
            rows = slice(g * B, (g + 1) * B)
            out = pieces[d][ROWS + g * B : ROWS + (g + 1) * B, :]
            prod = grad_ref[i, rows, :].astype(F32) * out.astype(F32)
            stat_ref[i, 0:1, rows] = jnp.sum(prod.T, axis=0, keepdims=True)
            stat_ref[i, 1:2, rows] = lse[g : g + 1]


def weigh(keys, vals, q_ref, grad_ref, stat_ref, i, allow, prob_ref, ds_ref):
    q = q_ref[i]
    grad = grad_ref[i]
    prob = jnp.exp2(nt(keys, q) * SCALE - stat_ref[i, 1:2, :])
    if allow is not None:
        prob = jnp.where(allow, prob, 0.0)
    diff = nt(vals, grad) - stat_ref[i, 0:1, :]
    prob_ref[...] = prob.astype(BF16)
    ds_ref[...] = (prob * diff).astype(BF16)


MS = sum(m << (2 * t) for t, m in enumerate((0, 0, 0, 1, 1, 2, 0, 1, 2, 3)))
QS = sum(i << (2 * t) for t, i in enumerate((1, 2, 3, 2, 3, 3, 0, 1, 2, 3)))


def make_own(dist, first, last):
    def kernel(q_ref, grad_ref, stat_ref, km_ref, ko_ref, *refs):
        if not first:
            dq_in, refs = refs[0], refs[1:]
        dm_ref, do_ref, refs = refs[0], refs[1], refs[2:]
        if last:
            dq_outs, refs = refs[:4], refs[4:]
            kt_ref, dk_ref, dv_ref, p0, s0, p1, s1, acc_ref = refs
        else:
            acc_ref, kt_ref, dk_ref, dv_ref, p0, s0, p1, s1 = refs
        chip = lax.axis_index("x")
        core = lax.axis_index("c")
        y = lax.axis_index("y")
        if first:
            acc_ref[...] = jnp.zeros_like(acc_ref)
        elif last:
            acc_ref[...] = dq_in[...]
        dk_ref[...] = jnp.zeros_like(dk_ref)
        dv_ref[...] = jnp.zeros_like(dv_ref)
        for m in range(4):
            kt_ref[m] = jnp.concatenate([km_ref[m, 0], ko_ref[m, 0]], axis=0).T
        if dist == 0:
            count = 10
        else:
            count = jnp.where(lax.rem(chip + 4 - dist, 4) < chip, 10, 6)

        def which(t):
            t = jnp.minimum(t, count - 1)
            m = lax.shift_right_logical(jnp.int32(MS), 2 * t) & 3
            i = lax.shift_right_logical(jnp.int32(QS), 2 * t) & 3
            return m, i, (y - m) & 3

        def before(t, prob_ref, ds_ref):
            m, i, slot = which(t)
            keys = jnp.concatenate([km_ref[slot, 0], ko_ref[slot, 0]], axis=0)
            vals = jnp.concatenate([km_ref[slot, 1], ko_ref[slot, 1]], axis=0)
            allow = None
            if dist == 0:
                row = lax.broadcasted_iota(jnp.int32, (2 * B, ROWS), 0)
                col = lax.broadcasted_iota(jnp.int32, (1, ROWS), 1)
                row = jnp.where(core == 0, row, row ^ B)
                allow = row <= core * B + col % B + jnp.where(i > m, 4 * B, 0)
            weigh(keys, vals, q_ref, grad_ref, stat_ref, i, allow, prob_ref, ds_ref)

        def after(t, prob_ref, ds_ref):
            _, i, slot = which(t)
            dv_ref[slot] += nn(prob_ref[...], grad_ref[i])
            dk_ref[slot] += nn(ds_ref[...], q_ref[i])
            acc_ref[i] += nn(kt_ref[slot], ds_ref[...])

        before(0, p0, s0)

        def two(u, carry):
            before(2 * u + 1, p1, s1)
            after(2 * u, p0, s0)
            before(2 * u + 2, p0, s0)
            after(2 * u + 1, p1, s1)
            return carry

        lax.fori_loop(0, count // 2, two, 0)
        for m in range(4):
            dk = (dk_ref[m] * FACTOR).astype(BF16)
            dv = dv_ref[m].astype(BF16)
            dm_ref[m, 0] = dk[:B]
            dm_ref[m, 1] = dv[:B]
            do_ref[m, 0] = dk[B:]
            do_ref[m, 1] = dv[B:]
        if last:
            for d in range(4):
                dq_outs[d][...] = (acc_ref[(y - d) & 3].T * FACTOR).astype(BF16)

    kv = shape((4, 2, B, HD), BF16)
    dq = [shape((ROWS, HD), BF16)] * 4 if last else [shape((4, HD, ROWS), F32)]
    scratch = [
        pltpu.VMEM((4, HD, 2 * B), BF16),
        pltpu.VMEM((4, 2 * B, HD), F32),
        pltpu.VMEM((4, 2 * B, HD), F32),
    ] + [pltpu.VMEM((2 * B, ROWS), BF16)] * 4
    if last:
        scratch.append(pltpu.VMEM((4, HD, ROWS), F32))
    aliases = None if first or last else {5: 2}
    return call(kernel, (kv, kv, *dq), 0, 5 if first else 6, scratch, aliases)


def sibling_kernel(len_ref, q_ref, grad_ref, stat_ref, mark_ref, dq_in, *refs):
    cur, prev, refs = refs[0:3], refs[3:6], refs[6:]
    dcur, dprev, acc_ref, k_ref, v_ref, list_ref, p0, s0, p1, s1 = refs
    thinker = lax.axis_index("z")
    y = lax.axis_index("y")
    shard = 2 * lax.axis_index("x") + lax.axis_index("c")
    length = len_ref[thinker]
    del dq_in
    dcur[...] = jnp.zeros_like(dcur)
    dprev[...] = jnp.zeros_like(dprev)
    step = (shard == 0).astype(jnp.int32)
    count = jnp.int32(0)
    for i in range(4):
        slot = (y - i) & 3
        old = (slot + step) & 3
        block = 8 * i + shard
        for n in range(3):
            code = i * 4 + n
            k_ref[code, :B] = prev[n][old, 0]
            k_ref[code, B:] = cur[n][slot, 0]
            v_ref[code, :B] = prev[n][old, 1]
            v_ref[code, B:] = cur[n][slot, 1]
            top = len_ref[(thinker - 1 - n) & 3] - (block - 1) * B
            wanted = jnp.max(mark_ref[i, 6 - n : 7 - n, :]) > 0.5
            list_ref[count] = code
            count = count + (wanted & (block * B < length) & (top > 0)).astype(jnp.int32)
    list_ref[count] = 0
    list_ref[count + 1] = 0
    list_ref[count + 2] = 0

    def before(t, prob_ref, ds_ref):
        code = list_ref[t]
        i, n = code // 4, code & 3
        block = 8 * i + shard
        top = len_ref[(thinker - 1 - n) & 3] - (block - 1) * B
        low = jnp.where(block == 0, B, 0)
        top = jnp.where(t < count, top, 0)
        row = lax.broadcasted_iota(jnp.int32, (2 * B, ROWS), 0)
        col = lax.broadcasted_iota(jnp.int32, (1, ROWS), 1) % B
        allow = (row > jnp.maximum(col, low - 1)) & (row <= jnp.minimum(col + B, top - 1))
        weigh(k_ref[code], v_ref[code], q_ref, grad_ref, stat_ref, i, allow, prob_ref, ds_ref)

    def after(t, prob_ref, ds_ref):
        code = list_ref[t]
        i, n = code // 4, code & 3
        slot = (y - i) & 3
        old = (slot + step) & 3
        dv = nn(prob_ref[...], grad_ref[i])
        dk = nn(ds_ref[...], q_ref[i]) * FACTOR
        acc_ref[i] += nn(k_ref[code].T, ds_ref[...])
        for kind, grad in ((0, dk), (1, dv)):
            dprev[n, old, kind] = (dprev[n, old, kind].astype(F32) + grad[:B]).astype(BF16)
            dcur[n, slot, kind] = (dcur[n, slot, kind].astype(F32) + grad[B:]).astype(BF16)

    @pl.when(count > 0)
    def _():
        before(0, p0, s0)

        def two(u, carry):
            before(2 * u + 1, p1, s1)
            after(2 * u, p0, s0)
            before(2 * u + 2, p0, s0)
            after(2 * u + 1, p1, s1)
            return carry

        lax.fori_loop(0, (count + 1) // 2, two, 0)


def merge(cur_ref, late_ref, *outs):
    for n in range(3):
        outs[n][...] = (cur_ref[n].astype(F32) + late_ref[n].astype(F32)).astype(BF16)


def gather_terms(*refs):
    terms, outs = refs[:-4], refs[-4:]
    for slot in range(4):
        total = terms[0][slot].astype(F32)
        for term in terms[1:]:
            total = total + term[slot].astype(F32)
        outs[slot][...] = total.astype(BF16)


def finish_q(d0, d1, d2, d3, out):
    y = lax.axis_index("y")
    for d, ref in enumerate((d0, d1, d2, d3)):
        head = lax.rem(y + d, 4)
        for g in range(GROUP):
            cols = pl.ds(pl.multiple_of((head * GROUP + g) * HD, HD), HD)
            out[:, cols] = ref[g * B : (g + 1) * B, :]


def finish_kv(d0, d1, d2, d3, k_out, v_out):
    y = lax.axis_index("y")
    for d, ref in enumerate((d0, d1, d2, d3)):
        cols = pl.ds(pl.multiple_of(lax.rem(y + d, 4) * HD, HD), HD)
        k_out[:, cols] = ref[0]
        v_out[:, cols] = ref[1]


def ring(x, axis, step, count):
    return lax.ppermute(x, axis, [(j, (j + step) % count) for j in range(count)])


def step(queries, keys, values, forward_out, logsumexp, upstream, lengths, sibling_mask):
    kv = shape((4, 2, B, HD), BF16)
    piece = shape((2, B, HD), BF16)
    row = shape((B, 512), BF16)
    core = ("x", "c")
    dists = (1, 2, 3)
    kv_sent = call(prep_kv, (piece,) * 4, 0, 2)(keys[0], values[0])
    kv_own = jnp.stack([kv_sent[0]] + [ring(kv_sent[d], "y", d, 4) for d in dists])
    qo_sent = call(prep_qo, (shape((QO, HD), BF16),) * 4, 1, 3)(
        sibling_mask.reshape(3), queries[0], forward_out[0], logsumexp.reshape(4, GROUP, B)
    )
    qo = [qo_sent[0]] + [ring(qo_sent[d], "y", d, 4) for d in dists]
    near = {0: kv_own, 1: ring(kv_own, "x", 1, 4), 3: ring(kv_own, "x", -1, 4)}
    near[2] = ring(near[3], "x", -1, 4)
    cur = [ring(kv_own, "z", d, 4) for d in dists]
    dealt = pl.pallas_call(
        deal,
        grid=(4,),
        out_shape=shape((128, 16, HD), BF16),
        in_specs=[pl.BlockSpec((32, 2048), lambda t: (t, 0))],
        out_specs=pl.BlockSpec((32, 16, HD), lambda t: (t, 0, 0)),
        scratch_shapes=[pltpu.VMEM((32, 16, HD), F32)],
        name="deal",
    )(upstream.reshape(128, 2048))
    arrived = lax.all_to_all(dealt, ("z", "y", "x", "c"), 0, 0, tiled=True)
    far = [ring(near[d], "c", 1, 2) for d in range(4)]
    prev = [ring(k, core, 1, 8) for k in cur]
    rows4 = shape((4, ROWS, HD), BF16)
    grads = call(unpack, rows4, 0, 1, [pltpu.VMEM((128, 16, HD), F32)])(arrived)
    query, stat, mark = call(
        prepare, (rows4, shape((4, 2, ROWS), F32), shape((4, 8, HD), F32)), 1, 5
    )(lengths, grads, *qo)
    rows_in = (query, grads, stat)
    mine, other, dq = {}, {}, None
    mine[3], other[3], dq = make_own(3, True, False)(*rows_in, near[3], far[3])
    mine[2], other[2], dq = make_own(2, False, False)(*rows_in, near[2], far[2], dq)
    trio = shape((3, 4, 2, B, HD), BF16)
    scratch = [pltpu.VMEM((16, 2 * B, HD), BF16)] * 2 + [pltpu.SMEM((16,), jnp.int32)]
    scratch += [pltpu.VMEM((2 * B, ROWS), BF16)] * 4
    sibling = call(sibling_kernel, (trio, trio, shape((4, HD, ROWS), F32)), 1, 11, scratch, {5: 2})
    dcur, dprev, dq = sibling(lengths, *rows_in, mark, dq, *cur, *prev)
    mine[1], other[1], dq = make_own(1, False, False)(*rows_in, near[1], far[1], dq)
    mine[0], other[0], *dq_sent = make_own(0, False, True)(*rows_in, near[0], far[0], dq)
    terms = [mine[0], ring(other[0], "c", 1, 2)]
    moved = {d: ring(other[d], "c", 1, 2).astype(F32) for d in dists}
    passing = ring((mine[2].astype(F32) + moved[2]).astype(BF16), "x", 1, 4)
    joined = (mine[3].astype(F32) + moved[3] + passing.astype(F32)).astype(BF16)
    nearest = (mine[1].astype(F32) + moved[1]).astype(BF16)
    terms.append(ring(joined, "x", 1, 4))
    terms.append(ring(nearest, "x", -1, 4))
    late = ring(dprev, core, -1, 8)
    merged = call(merge, (kv,) * 3, 0, 2)(dcur, late)
    terms += [ring(merged[d - 1], "z", -d, 4) for d in dists]
    dq_got = [dq_sent[0]] + [ring(dq_sent[d], "y", -d, 4) for d in dists]
    q_grad = call(finish_q, (shape((B, 2048), BF16),), 0, 4)(*dq_got)[0]
    kv_out = call(gather_terms, (piece,) * 4, 0, 7)(*terms)
    kv_got = [kv_out[0]] + [ring(kv_out[d], "y", -d, 4) for d in dists]
    k_grad, v_grad = call(finish_kv, (row, row), 0, 4)(*kv_got)
    return q_grad[None], k_grad[None], v_grad[None]


def solution(mesh):
    grid = Mesh(mesh.devices.reshape(4, 4, 4, 2), ("z",) + SEQ)
    rows = P("z", SEQ, None)
    return jax.shard_map(
        step,
        mesh=grid,
        in_specs=(
            rows,
            rows,
            rows,
            rows,
            P("z", None, SEQ),
            P(None, ("z",) + SEQ, None),
            P(),
            P("z", None, SEQ),
        ),
        out_specs=(rows, rows, rows),
        check_vma=False,
    )
```
